128 devices in a mesh: row: 8 (over x_hi, y), col: 16 (over z, x_lo, core).
Axes of the slice: x: 4 (x_hi: 2, x_lo: 2; x = x_hi * 2 + x_lo), y: 4, z: 4, core: 2. Of those that a mesh axis runs over, the one named last changes fastest.
Arguments:
- object_one: float32 [2, 2048, 4096], P(None, 'row', 'col'), may hold values from -5 to 5
- object_two: float32 [2, 2048, 4096], P(None, 'row', 'col'), may hold values from -5 to 5
- probe: float32 [2, 256, 256], replicated, may hold values from -6 to 6
- scan_pos: int32 [8, 16, 8, 2], P('row', 'col'), may hold values from 0 to 255
- pattern_index: int32 [8, 16, 8], P('row', 'col'), may hold values from 0 to 7, each once within a row
- measured: float32 [8, 16, 8, 256, 256], P('row', 'col'), may hold values from 0 to 3
Outputs:
- grad_one: float32 [2, 2048, 4096], P(None, 'row', 'col')
- grad_two: float32 [2, 2048, 4096], P(None, 'row', 'col')
- probe_step: float32 [2, 256, 256], replicated
The draws below stay inside these ranges and needn't reach their ends.
Inputs may be any that keep to these rules, and one draw needn't show every extreme that they name: For each tile (r, c), pattern_index[r, c] names each of that tile's 8 patterns exactly once.
All inputs are finite; a program needn't handle non-finite values.
Results may differ from the reference program's by a relative error of at most 0.00015.
Values sent between devices are 32-bit elements; how exact they have to be, the bound alone decides.
No kernel may reach another device: no remote copies, remote signals or barrier semaphores. Data moves between devices by JAX's collectives and lax.ppermute only.
A program may use at most 128 MiB of HBM per device.

```python
import jax
import jax.numpy as jnp
from jax import lax

WIN = 256
TILE = 256
POS = 8
TILE_ROWS = 8
TILE_COLS = 16
HEIGHT = 2048
WIDTH = 4096


def set_ends(drawn, stream_key, smallest, largest):
    longest = drawn.shape.index(max(drawn.shape))
    spots = []
    for shift in (0, 1):
        where = [jax.random.randint(jax.random.fold_in(stream_key, axis), (), 0, length) for axis, length in enumerate(drawn.shape)]
        where[longest] = (where[longest] + shift) % drawn.shape[longest]
        spots.append(tuple(where))
    return drawn.at[spots[0]].set(smallest).at[spots[1]].set(largest)


def steps_of(stream_key, dims, pieces, least, top_value):
    loudness = 1.0
    for axis_at, blocks in pieces:
        heights = jax.random.uniform(jax.random.fold_in(jax.random.fold_in(stream_key, 6), axis_at), (blocks,), jnp.float32, least / len(pieces), top_value / len(pieces))
        loudness = loudness * jnp.repeat(jnp.exp(heights), dims[axis_at] // blocks).reshape((-1,) + (1,) * (len(dims) - 1 - axis_at))
    return loudness


def gaussian(key, dims, width, limit, pieces=(), held_as=jnp.bfloat16):
    array = width * jax.random.normal(key, dims, jnp.float32)
    if pieces:
        array = array * steps_of(key, dims, pieces, -0.22, 0.18)
    return jnp.clip(array, -limit, limit).astype(held_as)


def setup_inputs(seed: int = 0) -> dict:
    arg_keys = jax.random.split(jax.random.key(seed), 7)
    object_one = gaussian(arg_keys[0], (2, HEIGHT, WIDTH), 0.7, 5.0, ((1, 8), (2, 16)), jnp.float32)
    object_two = gaussian(arg_keys[1], (2, HEIGHT, WIDTH), 0.7, 5.0, ((1, 8), (2, 16)), jnp.float32)
    probe = gaussian(arg_keys[2], (2, WIN, WIN), 1.0, 6.0, (), jnp.float32)
    scan_pos = set_ends(jax.random.randint(arg_keys[3], (TILE_ROWS, TILE_COLS, POS, 2), 0, TILE), jax.random.fold_in(arg_keys[3], 1), 0, TILE - 1).astype(jnp.int32)
    pattern_index = jax.vmap(lambda own: jax.random.permutation(own, POS))(jax.random.split(arg_keys[4], TILE_ROWS * TILE_COLS)).reshape((TILE_ROWS, TILE_COLS, POS)).astype(jnp.int32)
    measured = jnp.clip(3.0 * jax.random.uniform(arg_keys[5], (TILE_ROWS, TILE_COLS, POS, WIN, WIN), jnp.float32) ** steps_of(arg_keys[5], (TILE_ROWS, TILE_COLS, POS, WIN, WIN), ((0, 8), (1, 16)), -0.2, 0.2), 0.0, 3.0)
    return dict(object_one=object_one, object_two=object_two, probe=probe, scan_pos=scan_pos, pattern_index=pattern_index, measured=measured)


phase_rate = 0.002

def fresnel(window, float_type):
    counter = jnp.arange(window, dtype=jnp.int32)
    frequency = jnp.where(counter < window // 2, counter, counter - window).astype(float_type)
    phases = -phase_rate * (frequency[:, None] ** 2 + frequency[None, :] ** 2)
    return (jnp.cos(phases), jnp.sin(phases))

def forward_dft(field):
    return jnp.fft.fft2(field, norm='ortho')

def inverse_dft(field):
    return jnp.fft.ifft2(field, norm='ortho')

def reference(object_one, object_two, probe, scan_pos, pattern_index, measured):
    float_type = probe.dtype
    rim_width = WIN // 2
    padding = ((0, 0), (rim_width, rim_width), (rim_width, rim_width))
    padded_one = jnp.pad(object_one, padding)
    padded_two = jnp.pad(object_two, padding)
    kernel_re, kernel_im = fresnel(WIN, float_type)
    kernel = lax.complex(kernel_re, kernel_im)
    probe_c = lax.complex(probe[0], probe[1])
    shape_all = (TILE_ROWS, TILE_COLS, POS)
    rows_index = jnp.broadcast_to(jnp.arange(TILE_ROWS, dtype=jnp.int32)[:, None, None], shape_all).reshape(-1)
    cols_index = jnp.broadcast_to(jnp.arange(TILE_COLS, dtype=jnp.int32)[None, :, None], shape_all).reshape(-1)
    slot_index = jnp.broadcast_to(jnp.arange(POS, dtype=jnp.int32)[None, None, :], shape_all).reshape(-1)
    start_rows = (rows_index * TILE + scan_pos[..., 0].reshape(-1)).astype(jnp.int32)
    start_cols = (cols_index * TILE + scan_pos[..., 1].reshape(-1)).astype(jnp.int32)
    zero_index = jnp.zeros((), jnp.int32)

    def one_position(carry, inputs):
        accum_one, accum_two, numerator, illumination = carry
        start_row, start_col, tile_row, tile_col, slot = inputs
        place = (zero_index, start_row, start_col)
        win_one = lax.dynamic_slice(padded_one, place, (2, WIN, WIN))
        win_two = lax.dynamic_slice(padded_two, place, (2, WIN, WIN))
        one_c = lax.complex(win_one[0], win_one[1])
        two_c = lax.complex(win_two[0], win_two[1])
        wave = probe_c * one_c
        propagated = inverse_dft(kernel * forward_dft(wave))
        far_field = forward_dft(propagated * two_c)
        magnitude = jnp.sqrt(jnp.real(far_field) ** 2 + jnp.imag(far_field) ** 2 + 1.0)
        amplitude = measured[tile_row, tile_col, pattern_index[tile_row, tile_col, slot]]
        factor = (magnitude - amplitude) / magnitude
        back_two = inverse_dft(factor * far_field)
        term_two = jnp.conj(propagated) * back_two
        back_one = inverse_dft(jnp.conj(kernel) * forward_dft(jnp.conj(two_c) * back_two))
        term_one = jnp.conj(probe_c) * back_one
        share = jnp.conj(one_c) * back_one
        current_one = lax.dynamic_slice(accum_one, place, (2, WIN, WIN))
        accum_one = lax.dynamic_update_slice(accum_one, current_one + jnp.stack([jnp.real(term_one), jnp.imag(term_one)]), place)
        current_two = lax.dynamic_slice(accum_two, place, (2, WIN, WIN))
        accum_two = lax.dynamic_update_slice(accum_two, current_two + jnp.stack([jnp.real(term_two), jnp.imag(term_two)]), place)
        numerator = numerator + jnp.stack([jnp.real(share), jnp.imag(share)])
        illumination = illumination + win_one[0] * win_one[0] + win_one[1] * win_one[1]
        return ((accum_one, accum_two, numerator, illumination), None)
    initial = (jnp.zeros(padded_one.shape, float_type), jnp.zeros(padded_two.shape, float_type), jnp.zeros((2, WIN, WIN), float_type), jnp.zeros((WIN, WIN), float_type))
    final, unused = lax.scan(one_position, initial, (start_rows, start_cols, rows_index, cols_index, slot_index))
    accum_one, accum_two, numerator, illumination = final
    grad_one = accum_one[:, rim_width:rim_width + HEIGHT, rim_width:rim_width + WIDTH]
    grad_two = accum_two[:, rim_width:rim_width + HEIGHT, rim_width:rim_width + WIDTH]
    probe_step = numerator * lax.rsqrt(illumination + 1.0)
    return (grad_one, grad_two, probe_step)
```

```python
import jax
import jax.numpy as jnp
import ml_dtypes
import numpy as np
from jax import lax
from jax.experimental import pallas as pl
from jax.experimental.pallas import tpu as pltpu
from jax.sharding import PartitionSpec as P

phase_rate = 0.002
win = 256
half = 128
positions = 8
rows_at_once = 16
f32 = jnp.float32
bf16 = jnp.bfloat16


def real_form(table):
    return np.block([[table.real, table.imag], [-table.imag, table.real]])


def split_table(table):
    high = table.astype(np.float32).astype(ml_dtypes.bfloat16)
    low = (table - high.astype(np.float64)).astype(ml_dtypes.bfloat16)
    return high, low


def factor_tables():
    counter = np.arange(win)
    frequency = np.where(counter < half, counter, counter - win)
    kernel = np.exp(-1j * phase_rate * frequency.astype(np.float64) ** 2)
    response = np.fft.ifft(kernel)
    circulant = response[(counter[:, None] - counter[None, :]) % win]
    first, second = circulant[:half, :half], circulant[:half, half:]
    n, k = np.arange(half)[:, None], np.arange(half)[None, :]
    even = np.exp(-2j * np.pi * ((2 * n * k) % win) / win) / 16.0
    odd = np.exp(-2j * np.pi * ((n * (2 * k + 1)) % win) / win) / 16.0
    return [real_form(t) for t in (0.5 * (first + second), 0.5 * (first - second), even, odd)]


def stacked_tables():
    factors = factor_tables()
    every = factors + [t.T for t in factors]
    right, left = [], []
    for table in every:
        high, low = split_table(table)
        right.append(np.concatenate([high, high, low], axis=0))
        left.append(np.concatenate([high, high, low], axis=1))
    return np.stack(left), np.stack(right)


def column_order():
    order = np.concatenate([np.arange(0, win, 2), np.arange(1, win, 2)])
    table = np.zeros((win, win), np.float32)
    table[order, np.arange(win)] = 1.0
    return np.stack([table, table.T]).astype(ml_dtypes.bfloat16)


def split3(value):
    high = value.astype(bf16)
    rest = value - high.astype(f32)
    middle = rest.astype(bf16)
    low = (rest - middle.astype(f32)).astype(bf16)
    return high, middle, low


def prepare_body(pattern_ref, starts_ref, measured_ref, probe_ref, order_ref, sorted_ref, rolled_ref):
    position = pl.program_id(0)
    by_column = sum(jnp.dot(part, order_ref[0], preferred_element_type=f32) for part in split3(measured_ref[0]))
    sorted_ref[0] = sum(jnp.dot(order_ref[1], part, preferred_element_type=f32) for part in split3(by_column))
    down = lax.rem(starts_ref[position, 0], 8)
    across = starts_ref[position, 1]
    for plane in range(2):
        rolled_ref[0, plane] = pltpu.roll(pltpu.roll(probe_ref[plane], down, axis=0), across, axis=1)


def prepare(pattern, starts, measured, probe):
    order = jnp.asarray(column_order())
    return pl.pallas_call(
        prepare_body,
        out_shape=(
            jax.ShapeDtypeStruct((positions, win, win), f32),
            jax.ShapeDtypeStruct((positions, 2, win, win), f32),
        ),
        grid_spec=pltpu.PrefetchScalarGridSpec(
            num_scalar_prefetch=2,
            grid=(positions,),
            in_specs=[
                pl.BlockSpec((1, win, win), lambda j, pattern, starts: (pattern[j], 0, 0)),
                pl.BlockSpec((2, win, win), lambda j, pattern, starts: (0, 0, 0)),
                pl.BlockSpec((2, win, win), lambda j, pattern, starts: (0, 0, 0)),
            ],
            out_specs=[
                pl.BlockSpec((1, win, win), lambda j, pattern, starts: (j, 0, 0)),
                pl.BlockSpec((1, 2, win, win), lambda j, pattern, starts: (j, 0, 0, 0)),
            ],
        ),
        cost_estimate=pl.CostEstimate(flops=2 * 6 * positions * win**3, bytes_accessed=8 << 20, transcendentals=0),
        name="prepare",
    )(pattern, starts, measured, probe, order)


def complex_mul(left_re, left_im, right_re, right_im):
    return (left_re * right_re - left_im * right_im, left_re * right_im + left_im * right_re)


def conj_mul(left_re, left_im, right_re, right_im):
    return (left_re * right_re + left_im * right_im, left_re * right_im - left_im * right_re)


def put_left(ref, side, row, value):
    high = value.astype(bf16)
    low = (value - high.astype(f32)).astype(bf16)
    size = value.shape[0]
    ref[side, row : row + size, :] = high
    ref[side, win + row : win + row + size, :] = low
    ref[side, 2 * win + row : 2 * win + row + size, :] = high


def put_right(ref, side, row, lane, value):
    high = value.astype(bf16)
    low = (value - high.astype(f32)).astype(bf16)
    size = value.shape[0]
    ref[side, row : row + size, lane : lane + half] = high
    ref[side, row : row + size, win + lane : win + lane + half] = low
    ref[side, row : row + size, 2 * win + lane : 2 * win + lane + half] = high


def core_body(
    starts_ref,
    own_ref, left_ref, right_ref, top_ref, bottom_ref,
    rolled_ref, sorted_ref, ltab_ref, rtab_ref,
    out_top, out_mid, out_bottom, share_ref,
    wide, total, xa, xb, res, phi, shares,
):
    step = pl.program_id(0)
    R = rows_at_once

    @pl.when(step == 0)
    def _():
        wide[:, 0:half, :] = top_ref[...]
        wide[:, half + win : 2 * win, :] = bottom_ref[...]
        wide[:, half : half + win, 0:half] = left_ref[...]
        wide[:, half : half + win, half : half + win] = own_ref[...]
        wide[:, half : half + win, half + win :] = right_ref[...]
        total[...] = jnp.zeros_like(total)
        share_ref[...] = jnp.zeros_like(share_ref)

    a = starts_ref[step, 0]
    b = starts_ref[step, 1]
    offset = lax.rem(a, 8)
    base = pl.multiple_of(a - offset, 8)
    lanes = lax.broadcasted_iota(jnp.int32, (R, win), 1)
    near = lanes >= b
    below = lax.broadcasted_iota(jnp.int32, (R, win), 0) >= offset

    def row_sets(row):
        first = (pl.ds(base + row, R), None)
        return (first,) if row else (first, (pl.ds(base + win, R), below))

    def window(plane, row):
        value = None
        for rows, mask in row_sets(row):
            block = jnp.where(near, wide[plane, rows, 0:win], wide[plane, rows, win : 2 * win])
            value = block if mask is None else jnp.where(mask, value, block)
        return value

    def add_window(plane, row, value):
        zero = jnp.zeros_like(value)
        for rows, mask in row_sets(row):
            part = value
            if row == 0:
                part = jnp.where(below, value, zero) if mask is None else jnp.where(below, zero, value)
            total[plane, rows, 0:win] += jnp.where(near, part, zero)
            total[plane, rows, win : 2 * win] += jnp.where(near, zero, part)

    def left_stage(first):
        for side in range(2):
            res[side] = jnp.dot(ltab_ref[first + side], xa[side], preferred_element_type=f32)

    def right_stage(first):
        for side in range(2):
            res[side] = jnp.dot(xb[side], rtab_ref[first + side], preferred_element_type=f32)

    def row_butterfly(row, upper, lower):
        for part in range(2):
            put_left(xa, 0, part * half + row, upper[part] + lower[part])
            put_left(xa, 1, part * half + row, upper[part] - lower[part])

    def lane_butterfly(row, field):
        for part in range(2):
            near_half, far_half = field[part][:, :half], field[part][:, half:]
            put_right(xb, 0, row, part * half, near_half + far_half)
            put_right(xb, 1, row, part * half, near_half - far_half)

    def lane_join(row):
        out = []
        for part in range(2):
            plus = res[0, row : row + R, part * half : (part + 1) * half]
            minus = res[1, row : row + R, part * half : (part + 1) * half]
            out.append(jnp.concatenate([plus + minus, plus - minus], axis=1))
        return out

    def row_join(row):
        plus = [res[0, part * half + row : part * half + row + R, :] for part in range(2)]
        minus = [res[1, part * half + row : part * half + row + R, :] for part in range(2)]
        return [p + m for p, m in zip(plus, minus)], [p - m for p, m in zip(plus, minus)]

    def circulant(first_left, first_right):
        left_stage(first_left)
        for row in range(0, half, R):
            upper, lower = row_join(row)
            lane_butterfly(row, upper)
            lane_butterfly(half + row, lower)
        right_stage(first_right)

    def add_share(plane, value):
        value = pltpu.roll(value, jnp.where(offset == 0, 0, win - offset), axis=0)
        share_ref[plane] += pltpu.roll(value, jnp.where(b == 0, 0, win - b), axis=1)

    for row in range(0, half, R):
        pair = []
        for at in (row, half + row):
            o_re, o_im = window(0, at), window(1, at)
            shares[0, at : at + R, :] = o_re * o_re + o_im * o_im
            pair.append(complex_mul(rolled_ref[0, 0, at : at + R, :], rolled_ref[0, 1, at : at + R, :], o_re, o_im))
        row_butterfly(row, *pair)
    add_share(2, shares[0])
    circulant(4, 0)
    for row in range(0, half, R):
        pair = []
        for at in (row, half + row):
            p_re, p_im = lane_join(at)
            phi[0, at : at + R, :] = p_re
            phi[1, at : at + R, :] = p_im
            pair.append(complex_mul(p_re, p_im, window(2, at), window(3, at)))
        row_butterfly(row, *pair)
    left_stage(6)
    for side in range(2):
        for row in range(0, half, R):
            lane_butterfly(side * half + row, [res[side, part * half + row : part * half + row + R, :] for part in range(2)])
    right_stage(2)
    for side in range(2):
        for row in range(0, win, R):
            far_re = res[side, row : row + R, 0:half]
            far_im = res[side, row : row + R, half:win]
            amplitude = sorted_ref[0, row : row + R, side * half : (side + 1) * half]
            factor = 1.0 - amplitude * lax.rsqrt(far_re * far_re + far_im * far_im + 1.0)
            put_right(xb, side, row, 0, factor * far_re)
            put_right(xb, side, row, half, factor * far_im)
    right_stage(6)
    for side in range(2):
        for row in range(0, half, R):
            field = lane_join(side * half + row)
            for part in range(2):
                put_left(xa, side, part * half + row, field[part])
    left_stage(2)
    for row in range(0, half, R):
        pair = []
        for at, (g_re, g_im) in zip((row, half + row), row_join(row)):
            t_re, t_im = conj_mul(phi[0, at : at + R, :], phi[1, at : at + R, :], g_re, g_im)
            add_window(2, at, t_re)
            add_window(3, at, t_im)
            pair.append(conj_mul(window(2, at), window(3, at), g_re, g_im))
        row_butterfly(row, *pair)
    circulant(0, 4)
    for at in range(0, win, R):
        g_re, g_im = lane_join(at)
        t_re, t_im = conj_mul(rolled_ref[0, 0, at : at + R, :], rolled_ref[0, 1, at : at + R, :], g_re, g_im)
        add_window(0, at, t_re)
        add_window(1, at, t_im)
        s_re, s_im = conj_mul(window(0, at), window(1, at), g_re, g_im)
        shares[0, at : at + R, :] = s_re
        shares[1, at : at + R, :] = s_im
    add_share(0, shares[0])
    add_share(1, shares[1])

    @pl.when(step == positions - 1)
    def _():
        out_top[...] = total[:, 0:half, :]
        out_mid[...] = total[:, half : half + win, :]
        out_bottom[...] = total[:, half + win : 2 * win, :]


def core(starts, own, left, right, top, bottom, rolled, ordered):
    ltab, rtab = (jnp.asarray(t) for t in stacked_tables())
    whole = lambda *shape: pl.BlockSpec(shape, lambda j, starts: (0,) * len(shape))
    return pl.pallas_call(
        core_body,
        out_shape=(
            jax.ShapeDtypeStruct((4, half, 2 * win), f32),
            jax.ShapeDtypeStruct((4, win, 2 * win), f32),
            jax.ShapeDtypeStruct((4, half, 2 * win), f32),
            jax.ShapeDtypeStruct((3, win, win), f32),
        ),
        grid_spec=pltpu.PrefetchScalarGridSpec(
            num_scalar_prefetch=1,
            grid=(positions,),
            in_specs=[
                whole(4, win, win), whole(4, win, half), whole(4, win, half),
                whole(4, half, 2 * win), whole(4, half, 2 * win),
                pl.BlockSpec((1, 2, win, win), lambda j, starts: (j, 0, 0, 0)),
                pl.BlockSpec((1, win, win), lambda j, starts: (j, 0, 0)),
                whole(8, win, 3 * win), whole(8, 3 * win, win),
            ],
            out_specs=[
                whole(4, half, 2 * win), whole(4, win, 2 * win), whole(4, half, 2 * win), whole(3, win, win),
            ],
            scratch_shapes=[
                pltpu.VMEM((4, 2 * win + 8, 2 * win), f32),
                pltpu.VMEM((4, 2 * win + 8, 2 * win), f32),
                pltpu.VMEM((2, 3 * win, win), bf16),
                pltpu.VMEM((2, win, 3 * win), bf16),
                pltpu.VMEM((2, win, win), f32),
                pltpu.VMEM((2, win, win), f32),
                pltpu.VMEM((2, win, win), f32),
            ],
        ),
        compiler_params=pltpu.CompilerParams(vmem_limit_bytes=60 << 20),
        cost_estimate=pl.CostEstimate(flops=48 * 2 * positions * win**3, bytes_accessed=32 << 20, transcendentals=0),
        name="core",
    )(starts, own, left, right, top, bottom, rolled, ordered, ltab, rtab)


def shifted(block, axis, distance):
    size = lax.axis_size(axis)
    return lax.ppermute(block, axis, [(i, i + distance) for i in range(size) if 0 <= i + distance < size])


def summed_step(share):
    devices = lax.axis_size("row") * lax.axis_size("col")
    rows = win // devices
    pieces = share.reshape(3, devices, rows * win // half, half).transpose(1, 0, 2, 3)
    pieces = pieces.reshape(devices, 3 * rows * win // half, half)
    pieces = lax.all_to_all(pieces, ("row", "col"), 0, 0, tiled=True)
    piece = jnp.sum(pieces, axis=0).reshape(3, rows * win // half, half)
    step = piece[:2] * lax.rsqrt(piece[2:] + 1.0)
    flat = step.reshape(1, 2 * rows * win // half, half)
    every = lax.all_to_all(jnp.broadcast_to(flat, (devices,) + flat.shape[1:]), ("row", "col"), 0, 0, tiled=True)
    every = every.reshape(devices, 2, rows * win // half, half).transpose(1, 0, 2, 3)
    return every.reshape(2, win, win)


def body(object_one, object_two, probe, scan_pos, pattern_index, measured):
    starts = scan_pos[0, 0]
    own = jnp.concatenate([object_one, object_two], axis=0)
    left = shifted(own[:, :, half:], "col", 1)
    right = shifted(own[:, :, :half], "col", -1)
    below = jnp.concatenate([left[:, half:], own[:, half:], right[:, half:]], axis=2)
    above = jnp.concatenate([left[:, :half], own[:, :half], right[:, :half]], axis=2)
    top = shifted(below, "row", 1)
    bottom = shifted(above, "row", -1)
    ordered, rolled = prepare(pattern_index[0, 0], starts, measured[0, 0], probe)
    out_top, out_mid, out_bottom, share = core(starts, own, left, right, top, bottom, rolled, ordered)
    from_below = shifted(out_top, "row", -1)
    from_above = shifted(out_bottom, "row", 1)
    mid = jnp.concatenate([out_mid[:, :half] + from_above, out_mid[:, half:] + from_below], axis=1)
    from_after = shifted(mid[:, :, :half], "col", -1)
    from_before = shifted(mid[:, :, half + win :], "col", 1)
    grad = jnp.concatenate([mid[:, :, half:win] + from_before, mid[:, :, win : win + half] + from_after], axis=2)
    return (grad[:2], grad[2:], summed_step(share))


def solution(mesh):
    placed = (
        P(None, "row", "col"),
        P(None, "row", "col"),
        P(),
        P("row", "col", None, None),
        P("row", "col", None),
        P("row", "col", None, None, None),
    )
    return jax.shard_map(
        body,
        mesh=mesh,
        in_specs=placed,
        out_specs=(P(None, "row", "col"), P(None, "row", "col"), P()),
        check_vma=False,
    )
```

```python
import math

import jax
import jax.numpy as jnp
import ml_dtypes
import numpy as np
from jax import lax
from jax.experimental import pallas as pl
from jax.experimental.pallas import tpu as pltpu
from jax.sharding import PartitionSpec as P

phase_rate = 0.002
win = 256
half = 128
positions = 8
rows_at_once = 16
at_once = 2
f32 = jnp.float32
bf16 = jnp.bfloat16


def real_form(table):
    return np.block([[table.real, table.imag], [-table.imag, table.real]])


def split_table(table):
    high = table.astype(np.float32).astype(ml_dtypes.bfloat16)
    low = (table - high.astype(np.float64)).astype(ml_dtypes.bfloat16)
    return high, low


def factor_tables():
    counter = np.arange(win)
    frequency = np.where(counter < half, counter, counter - win)
    kernel = np.exp(-1j * phase_rate * frequency.astype(np.float64) ** 2)
    response = np.fft.ifft(kernel)
    circulant = response[(counter[:, None] - counter[None, :]) % win]
    first, second = circulant[:half, :half], circulant[:half, half:]
    n, k = np.arange(half)[:, None], np.arange(half)[None, :]
    even = np.exp(-2j * np.pi * ((2 * n * k) % win) / win) / 16.0
    odd = np.exp(-2j * np.pi * ((n * (2 * k + 1)) % win) / win) / 16.0
    return [real_form(t) for t in (0.5 * (first + second), 0.5 * (first - second), even, odd)]


def table_parts():
    return np.stack([np.stack(split_table(table)) for table in factor_tables()])


def column_order():
    order = np.concatenate([np.arange(0, win, 2), np.arange(1, win, 2)])
    table = np.zeros((win, win), np.float32)
    table[order, np.arange(win)] = 1.0
    return np.stack([table, table.T]).astype(ml_dtypes.bfloat16)


def split3(value):
    high = value.astype(bf16)
    rest = value - high.astype(f32)
    middle = rest.astype(bf16)
    low = (rest - middle.astype(f32)).astype(bf16)
    return high, middle, low


def prepare_body(
    pattern_ref, starts_ref, measured_ref, probe_ref, order_ref, parts_ref,
    sorted_ref, rolled_ref, left_ref, right_ref,
):
    position = pl.program_id(0)
    by_column = sum(jnp.dot(part, order_ref[0], preferred_element_type=f32) for part in split3(measured_ref[0]))
    sorted_ref[0] = sum(jnp.dot(order_ref[1], part, preferred_element_type=f32) for part in split3(by_column))
    down = lax.rem(starts_ref[position, 0], 8)
    across = starts_ref[position, 1]
    for plane in range(2):
        rolled_ref[0, plane] = pltpu.roll(pltpu.roll(probe_ref[plane], down, axis=0), across, axis=1)
    turned = position >= 4
    for part, spots in ((0, (0, 1)), (1, (2,))):
        table = parts_ref[0, part].astype(f32)
        table = jnp.where(turned, table.T, table).astype(bf16)
        for spot in spots:
            left_ref[0, :, spot * win : (spot + 1) * win] = table
            right_ref[0, spot * win : (spot + 1) * win, :] = table


def prepare(pattern, starts, measured, probe):
    order = jnp.asarray(column_order())
    parts = jnp.asarray(table_parts())
    return pl.pallas_call(
        prepare_body,
        out_shape=(
            jax.ShapeDtypeStruct((positions, win, win), f32),
            jax.ShapeDtypeStruct((positions, 2, win, win), f32),
            jax.ShapeDtypeStruct((8, win, 3 * win), bf16),
            jax.ShapeDtypeStruct((8, 3 * win, win), bf16),
        ),
        grid_spec=pltpu.PrefetchScalarGridSpec(
            num_scalar_prefetch=2,
            grid=(positions,),
            in_specs=[
                pl.BlockSpec((1, win, win), lambda j, pattern, starts: (pattern[j], 0, 0)),
                pl.BlockSpec((2, win, win), lambda j, pattern, starts: (0, 0, 0)),
                pl.BlockSpec((2, win, win), lambda j, pattern, starts: (0, 0, 0)),
                pl.BlockSpec((1, 2, win, win), lambda j, pattern, starts: (lax.rem(j, 4), 0, 0, 0)),
            ],
            out_specs=[
                pl.BlockSpec((1, win, win), lambda j, pattern, starts: (j, 0, 0)),
                pl.BlockSpec((1, 2, win, win), lambda j, pattern, starts: (j, 0, 0, 0)),
                pl.BlockSpec((1, win, 3 * win), lambda j, pattern, starts: (j, 0, 0)),
                pl.BlockSpec((1, 3 * win, win), lambda j, pattern, starts: (j, 0, 0)),
            ],
        ),
        cost_estimate=pl.CostEstimate(flops=2 * 6 * positions * win**3, bytes_accessed=16 << 20, transcendentals=0),
        name="prepare",
    )(pattern, starts, measured, probe, order, parts)


def complex_mul(left_re, left_im, right_re, right_im):
    return (left_re * right_re - left_im * right_im, left_re * right_im + left_im * right_re)


def conj_mul(left_re, left_im, right_re, right_im):
    return (left_re * right_re + left_im * right_im, left_re * right_im - left_im * right_re)


def put_left(ref, side, row, value):
    high = value.astype(bf16)
    low = (value - high.astype(f32)).astype(bf16)
    size = value.shape[0]
    ref[side, row : row + size, :] = high
    ref[side, win + row : win + row + size, :] = low
    ref[side, 2 * win + row : 2 * win + row + size, :] = high


def put_right(ref, side, row, lane, value):
    high = value.astype(bf16)
    low = (value - high.astype(f32)).astype(bf16)
    size = value.shape[0]
    ref[side, row : row + size, lane : lane + half] = high
    ref[side, row : row + size, win + lane : win + lane + half] = low
    ref[side, row : row + size, 2 * win + lane : 2 * win + lane + half] = high


def core_body(
    starts_ref, flags_ref,
    one_ref, two_ref, ca_ref, cb_ref, ra_ref, rb_ref,
    rolled_ref, sorted_ref, ltab_ref, rtab_ref,
    out_ra, out_rb, out_mid, out_keep, out_send,
    wide, total, share, *slots,
):
    step = pl.program_id(0)
    R = rows_at_once
    row_odd, col_odd = flags_ref[0], flags_ref[1]
    row_a = pl.multiple_of((1 - row_odd) * (win + half), half)
    row_b = pl.multiple_of(row_odd * (win + half), half)
    lane_a = pl.multiple_of((1 - col_odd) * (win + half), half)
    lane_b = pl.multiple_of(col_odd * (win + half), half)

    @pl.when(step == 0)
    def _():
        wide[:, pl.ds(row_a, half), :] = ra_ref[...]
        wide[:, pl.ds(row_b, half), :] = rb_ref[...]
        wide[:, half : half + win, pl.ds(lane_a, half)] = ca_ref[...]
        wide[:, half : half + win, pl.ds(lane_b, half)] = cb_ref[...]
        wide[0:2, half : half + win, half : half + win] = one_ref[...]
        wide[2:4, half : half + win, half : half + win] = two_ref[...]
        total[...] = jnp.zeros_like(total)
        share[...] = jnp.zeros_like(share)

    def work(slot):
        xa, xb, res, phi, shares = slots[5 * slot : 5 * slot + 5]
        position = at_once * step + slot
        a = starts_ref[position, 0]
        b = starts_ref[position, 1]
        offset = lax.rem(a, 8)
        base = pl.multiple_of(a - offset, 8)
        near = lax.broadcasted_iota(jnp.int32, (R, win), 1) >= b
        below = lax.broadcasted_iota(jnp.int32, (R, win), 0) >= offset

        def row_sets(row):
            first = (pl.ds(base + row, R), None)
            return (first,) if row else (first, (pl.ds(base + win, R), below))

        def window(plane, row):
            value = None
            for rows, mask in row_sets(row):
                block = jnp.where(near, wide[plane, rows, 0:win], wide[plane, rows, win : 2 * win])
                value = block if mask is None else jnp.where(mask, value, block)
            return value

        def add_window(plane, row, value):
            zero = jnp.zeros_like(value)
            for rows, mask in row_sets(row):
                part = value
                if row == 0:
                    part = jnp.where(below, value, zero) if mask is None else jnp.where(below, zero, value)
                total[plane, rows, 0:win] += jnp.where(near, part, zero)
                total[plane, rows, win : 2 * win] += jnp.where(near, zero, part)

        def left_stage(first):
            for side in range(2):
                res[side] = jnp.dot(ltab_ref[first + side], xa[side], preferred_element_type=f32)

        def right_stage(first):
            for side in range(2):
                res[side] = jnp.dot(xb[side], rtab_ref[first + side], preferred_element_type=f32)

        def row_butterfly(row, upper, lower):
            for part in range(2):
                put_left(xa, 0, part * half + row, upper[part] + lower[part])
                put_left(xa, 1, part * half + row, upper[part] - lower[part])

        def lane_butterfly(row, field):
            for part in range(2):
                near_half, far_half = field[part][:, :half], field[part][:, half:]
                put_right(xb, 0, row, part * half, near_half + far_half)
                put_right(xb, 1, row, part * half, near_half - far_half)

        def lane_join(row):
            out = []
            for part in range(2):
                plus = res[0, row : row + R, part * half : (part + 1) * half]
                minus = res[1, row : row + R, part * half : (part + 1) * half]
                out.append(jnp.concatenate([plus + minus, plus - minus], axis=1))
            return out

        def row_join(row):
            plus = [res[0, part * half + row : part * half + row + R, :] for part in range(2)]
            minus = [res[1, part * half + row : part * half + row + R, :] for part in range(2)]
            return [p + m for p, m in zip(plus, minus)], [p - m for p, m in zip(plus, minus)]

        def rows_to_lanes():
            for row in range(0, half, R):
                upper, lower = row_join(row)
                lane_butterfly(row, upper)
                lane_butterfly(half + row, lower)

        def add_share(plane, value):
            value = pltpu.roll(value, jnp.where(offset == 0, 0, win - offset), axis=0)
            share[plane] += pltpu.roll(value, jnp.where(b == 0, 0, win - b), axis=1)

        def probe(part, row):
            return rolled_ref[slot, part, row : row + R, :]

        for row in range(0, half, R):
            pair = []
            for at in (row, half + row):
                o_re, o_im = window(0, at), window(1, at)
                shares[0, at : at + R, :] = o_re * o_re + o_im * o_im
                pair.append(complex_mul(probe(0, at), probe(1, at), o_re, o_im))
            row_butterfly(row, *pair)
        yield
        left_stage(4)
        add_share(2, shares[0])
        yield
        rows_to_lanes()
        yield
        right_stage(0)
        yield
        for row in range(0, half, R):
            pair = []
            for at in (row, half + row):
                p_re, p_im = lane_join(at)
                phi[0, at : at + R, :] = p_re
                phi[1, at : at + R, :] = p_im
                pair.append(complex_mul(p_re, p_im, window(2, at), window(3, at)))
            row_butterfly(row, *pair)
        yield
        left_stage(6)
        yield
        for side in range(2):
            for row in range(0, half, R):
                lane_butterfly(
                    side * half + row, [res[side, part * half + row : part * half + row + R, :] for part in range(2)]
                )
        yield
        right_stage(2)
        yield
        for side in range(2):
            for row in range(0, win, R):
                far_re = res[side, row : row + R, 0:half]
                far_im = res[side, row : row + R, half:win]
                amplitude = sorted_ref[slot, row : row + R, side * half : (side + 1) * half]
                factor = 1.0 - amplitude * lax.rsqrt(far_re * far_re + far_im * far_im + 1.0)
                put_right(xb, side, row, 0, factor * far_re)
                put_right(xb, side, row, half, factor * far_im)
        yield
        right_stage(6)
        yield
        for side in range(2):
            for row in range(0, half, R):
                field = lane_join(side * half + row)
                for part in range(2):
                    put_left(xa, side, part * half + row, field[part])
        yield
        left_stage(2)
        yield
        for row in range(0, half, R):
            pair = []
            for at, (g_re, g_im) in zip((row, half + row), row_join(row)):
                t_re, t_im = conj_mul(phi[0, at : at + R, :], phi[1, at : at + R, :], g_re, g_im)
                add_window(2, at, t_re)
                add_window(3, at, t_im)
                pair.append(conj_mul(window(2, at), window(3, at), g_re, g_im))
            row_butterfly(row, *pair)
        yield
        left_stage(0)
        yield
        rows_to_lanes()
        yield
        right_stage(4)
        yield
        for at in range(0, win, R):
            g_re, g_im = lane_join(at)
            t_re, t_im = conj_mul(probe(0, at), probe(1, at), g_re, g_im)
            add_window(0, at, t_re)
            add_window(1, at, t_im)
            s_re, s_im = conj_mul(window(0, at), window(1, at), g_re, g_im)
            shares[0, at : at + R, :] = s_re
            shares[1, at : at + R, :] = s_im
        add_share(0, shares[0])
        add_share(1, shares[1])
        yield

    running = [work(slot) for slot in range(at_once)]
    live = []
    while running or live:
        if running:
            live.append(running.pop(0))
        live = [w for w in live if next(w, "end") is None]

    @pl.when(step == positions // at_once - 1)
    def _():
        out_ra[...] = total[:, pl.ds(row_a, half), :]
        out_rb[...] = total[:, pl.ds(row_b, half), :]
        out_mid[...] = total[:, half : half + win, :]
        out_keep[...] = share[:, pl.ds(pl.multiple_of(col_odd * half, half), half), :]
        out_send[...] = share[:, pl.ds(pl.multiple_of((1 - col_odd) * half, half), half), :]


def whole(*shape):
    return pl.BlockSpec(shape, lambda *ids: (0,) * len(shape))


def core(starts, flags, one, two, ca, cb, ra, rb, rolled, ordered, ltab, rtab):
    shapes = ((4, half, 2 * win), (4, half, 2 * win), (4, win, 2 * win), (3, half, win), (3, half, win))
    slot = [
        pltpu.VMEM((2, 3 * win, win), bf16),
        pltpu.VMEM((2, win, 3 * win), bf16),
        pltpu.VMEM((2, win, win), f32),
        pltpu.VMEM((2, win, win), f32),
        pltpu.VMEM((2, win, win), f32),
    ]
    return pl.pallas_call(
        core_body,
        out_shape=[jax.ShapeDtypeStruct(shape, f32) for shape in shapes],
        grid_spec=pltpu.PrefetchScalarGridSpec(
            num_scalar_prefetch=2,
            grid=(positions // at_once,),
            in_specs=[
                whole(2, win, win), whole(2, win, win), whole(4, win, half), whole(4, win, half),
                whole(4, half, 2 * win), whole(4, half, 2 * win),
                pl.BlockSpec((at_once, 2, win, win), lambda j, *prefetched: (j, 0, 0, 0)),
                pl.BlockSpec((at_once, win, win), lambda j, *prefetched: (j, 0, 0)),
                whole(8, win, 3 * win), whole(8, 3 * win, win),
            ],
            out_specs=[whole(*shape) for shape in shapes],
            scratch_shapes=[
                pltpu.VMEM((4, 2 * win + 8, 2 * win), f32),
                pltpu.VMEM((4, 2 * win + 8, 2 * win), f32),
                pltpu.VMEM((3, win, win), f32),
            ] + slot * at_once,
        ),
        compiler_params=pltpu.CompilerParams(vmem_limit_bytes=60 << 20),
        cost_estimate=pl.CostEstimate(flops=48 * 2 * positions * win**3, bytes_accessed=32 << 20, transcendentals=0),
        name="core",
    )(starts, flags, one, two, ca, cb, ra, rb, rolled, ordered, ltab, rtab)


def small_kernel(kernel, name, flags, inputs, shapes):
    size = sum(x.size for x in inputs) + sum(math.prod(shape) for shape in shapes)
    return pl.pallas_call(
        kernel,
        out_shape=[jax.ShapeDtypeStruct(shape, f32) for shape in shapes],
        grid_spec=pltpu.PrefetchScalarGridSpec(
            num_scalar_prefetch=1,
            grid=(1,),
            in_specs=[whole(*x.shape) for x in inputs],
            out_specs=[whole(*shape) for shape in shapes],
        ),
        compiler_params=pltpu.CompilerParams(vmem_limit_bytes=48 << 20),
        cost_estimate=pl.CostEstimate(flops=size, bytes_accessed=4 * size, transcendentals=0),
        name=name,
    )(flags, *inputs)


def half_at(choice):
    return pl.ds(pl.multiple_of(choice * half, half), half)


def pack_columns(flags_ref, one_ref, two_ref, a_ref, b_ref):
    odd = flags_ref[1]
    for out, lanes in ((a_ref, half_at(1 - odd)), (b_ref, half_at(odd))):
        out[0:2] = one_ref[:, :, lanes]
        out[2:4] = two_ref[:, :, lanes]


def pack_rows(flags_ref, one_ref, two_ref, ca_ref, cb_ref, a_ref, b_ref):
    row_odd, col_odd = flags_ref[0], flags_ref[1]
    for out, rows in ((a_ref, half_at(1 - row_odd)), (b_ref, half_at(row_odd))):
        out[0:2, :, half : half + win] = one_ref[:, rows, :]
        out[2:4, :, half : half + win] = two_ref[:, rows, :]
        out[:, :, half_at(3 * (1 - col_odd))] = ca_ref[:, rows, :]
        out[:, :, half_at(3 * col_odd)] = cb_ref[:, rows, :]


def fold_rows(flags_ref, mid_ref, qa_ref, qb_ref, a_ref, b_ref, center_ref):
    row_odd, col_odd = flags_ref[0], flags_ref[1]
    for got, rows in ((qa_ref, half_at(1 - row_odd)), (qb_ref, half_at(row_odd))):
        center_ref[:, rows, :] = mid_ref[:, rows, half : half + win] + got[:, :, half : half + win]
        for out, lanes in ((a_ref, half_at(3 * (1 - col_odd))), (b_ref, half_at(3 * col_odd))):
            out[:, rows, :] = mid_ref[:, rows, lanes] + got[:, :, lanes]


def fold_columns(flags_ref, center_ref, a_ref, b_ref, one_ref, two_ref):
    odd = flags_ref[1]
    for got, lanes in ((a_ref, half_at(1 - odd)), (b_ref, half_at(odd))):
        one_ref[:, :, lanes] = center_ref[0:2, :, lanes] + got[0:2]
        two_ref[:, :, lanes] = center_ref[2:4, :, lanes] + got[2:4]


def pack_share(flags_ref, keep_ref, got_ref, out_ref):
    for tile in range(64):
        for plane, spot in ((tile // 32, 0), (2, 8)):
            rows = slice(tile % 32 // 2 * 8, tile % 32 // 2 * 8 + 8)
            lanes = slice(tile % 2 * half, tile % 2 * half + half)
            out_ref[tile, spot : spot + 8, :] = keep_ref[plane, rows, lanes] + got_ref[plane, rows, lanes]


def take_step(flags_ref, parts_ref, out_ref):
    total = parts_ref[0]
    for tile in range(1, 64):
        total = total + parts_ref[tile]
    step = total[0:8] * lax.rsqrt(total[8:16] + 1.0)
    for tile in range(64):
        out_ref[tile] = step


def join_step(flags_ref, own_ref, other_ref, out_ref):
    odd = flags_ref[1]
    for tile in range(64):
        row = tile % 32 // 2 * 8
        lanes = slice(tile % 2 * half, tile % 2 * half + half)
        out_ref[tile // 32, pl.ds(pl.multiple_of(odd * half + row, 8), 8), lanes] = own_ref[tile]
        out_ref[tile // 32, pl.ds(pl.multiple_of((1 - odd) * half + row, 8), 8), lanes] = other_ref[tile]


def swapped(block, axis, first):
    pairs = [(i, i + 1) for i in range(first, lax.axis_size(axis) - 1, 2)]
    return lax.ppermute(block, axis, pairs + [(j, i) for i, j in pairs])


def exchanged(parts):
    rows, cols = lax.axis_size("row"), lax.axis_size("col")
    groups = [[r * cols + c for r in range(rows) for c in range(odd, cols, 2)] for odd in range(2)]
    return lax.all_to_all(parts, ("row", "col"), 0, 0, axis_index_groups=groups, tiled=True)


def body(object_one, object_two, probe, scan_pos, pattern_index, measured):
    starts = scan_pos[0, 0]
    flags = jnp.stack([lax.axis_index("row") % 2, lax.axis_index("col") % 2]).astype(jnp.int32)
    side, slab = (4, win, half), (4, half, 2 * win)
    ca, cb = small_kernel(pack_columns, "pack_columns", flags, (object_one, object_two), (side, side))
    ca, cb = swapped(ca, "col", 0), swapped(cb, "col", 1)
    ra, rb = small_kernel(pack_rows, "pack_rows", flags, (object_one, object_two, ca, cb), (slab, slab))
    ra, rb = swapped(ra, "row", 0), swapped(rb, "row", 1)
    ordered, rolled, ltab, rtab = prepare(pattern_index[0, 0], starts, measured[0, 0], probe)
    out_ra, out_rb, mid, keep, send = core(
        starts, flags, object_one, object_two, ca, cb, ra, rb, rolled, ordered, ltab, rtab
    )
    share = small_kernel(pack_share, "pack_share", flags, (keep, swapped(send, "col", 0)), ((64, 16, half),))[0]
    qa, qb = swapped(out_ra, "row", 0), swapped(out_rb, "row", 1)
    fa, fb, center = small_kernel(fold_rows, "fold_rows", flags, (mid, qa, qb), (side, side, (4, win, win)))
    ga, gb = swapped(fa, "col", 0), swapped(fb, "col", 1)
    step = small_kernel(take_step, "take_step", flags, (exchanged(share),), ((64, 8, half),))[0]
    step = exchanged(step)
    tile_shape = (2, win, win)
    grad_one, grad_two = small_kernel(fold_columns, "fold_columns", flags, (center, ga, gb), (tile_shape, tile_shape))
    probe_step = small_kernel(join_step, "join_step", flags, (step, swapped(step, "col", 0)), (tile_shape,))[0]
    return (grad_one, grad_two, probe_step)


def solution(mesh):
    placed = (
        P(None, "row", "col"),
        P(None, "row", "col"),
        P(),
        P("row", "col", None, None),
        P("row", "col", None),
        P("row", "col", None, None, None),
    )
    return jax.shard_map(
        body,
        mesh=mesh,
        in_specs=placed,
        out_specs=(P(None, "row", "col"), P(None, "row", "col"), P()),
        check_vma=False,
    )
```

```python
import math

import jax
import jax.numpy as jnp
import ml_dtypes
import numpy as np
from jax import lax
from jax.experimental import pallas as pl
from jax.experimental.pallas import tpu as pltpu
from jax.sharding import PartitionSpec as P

phase_rate = 0.002
win = 256
half = 128
positions = 8
rows_at_once = 16
at_once = 2
f32 = jnp.float32
bf16 = jnp.bfloat16


def real_form(table):
    return np.block([[table.real, table.imag], [-table.imag, table.real]])


def split_table(table):
    high = table.astype(np.float32).astype(ml_dtypes.bfloat16)
    low = (table - high.astype(np.float64)).astype(ml_dtypes.bfloat16)
    return high, low


def factor_tables():
    counter = np.arange(win)
    frequency = np.where(counter < half, counter, counter - win)
    kernel = np.exp(-1j * phase_rate * frequency.astype(np.float64) ** 2)
    response = np.fft.ifft(kernel)
    circulant = response[(counter[:, None] - counter[None, :]) % win]
    first, second = circulant[:half, :half], circulant[:half, half:]
    n, k = np.arange(half)[:, None], np.arange(half)[None, :]
    even = np.exp(-2j * np.pi * ((2 * n * k) % win) / win) / 16.0
    odd = np.exp(-2j * np.pi * ((n * (2 * k + 1)) % win) / win) / 16.0
    return [real_form(t) for t in (0.5 * (first + second), 0.5 * (first - second), even, odd)]


def table_parts():
    return np.stack([np.stack(split_table(table)) for table in factor_tables()])


def column_order():
    order = np.concatenate([np.arange(0, win, 2), np.arange(1, win, 2)])
    table = np.zeros((win, win), np.float32)
    table[order, np.arange(win)] = 1.0
    return np.stack([table, table.T]).astype(ml_dtypes.bfloat16)


def split3(value):
    high = value.astype(bf16)
    rest = value - high.astype(f32)
    middle = rest.astype(bf16)
    low = (rest - middle.astype(f32)).astype(bf16)
    return high, middle, low


def prepare_body(
    pattern_ref, starts_ref, measured_ref, probe_ref, order_ref, parts_ref,
    sorted_ref, rolled_ref, left_ref, right_ref,
):
    position = pl.program_id(0)
    by_column = sum(jnp.dot(part, order_ref[0], preferred_element_type=f32) for part in split3(measured_ref[0]))
    sorted_ref[0] = sum(jnp.dot(order_ref[1], part, preferred_element_type=f32) for part in split3(by_column))
    down = lax.rem(starts_ref[position, 0], 8)
    across = starts_ref[position, 1]
    for plane in range(2):
        rolled_ref[0, plane] = pltpu.roll(pltpu.roll(probe_ref[plane], down, axis=0), across, axis=1)
    turned = position >= 4
    for part, spots in ((0, (0, 1)), (1, (2,))):
        table = parts_ref[0, part].astype(f32)
        table = jnp.where(turned, table.T, table).astype(bf16)
        for spot in spots:
            left_ref[0, :, spot * win : (spot + 1) * win] = table
            right_ref[0, spot * win : (spot + 1) * win, :] = table


def prepare(pattern, starts, measured, probe):
    order = jnp.asarray(column_order())
    parts = jnp.asarray(table_parts())
    return pl.pallas_call(
        prepare_body,
        out_shape=(
            jax.ShapeDtypeStruct((positions, win, win), f32),
            jax.ShapeDtypeStruct((positions, 2, win, win), f32),
            jax.ShapeDtypeStruct((8, win, 3 * win), bf16),
            jax.ShapeDtypeStruct((8, 3 * win, win), bf16),
        ),
        grid_spec=pltpu.PrefetchScalarGridSpec(
            num_scalar_prefetch=2,
            grid=(positions,),
            in_specs=[
                pl.BlockSpec((1, win, win), lambda j, pattern, starts: (pattern[j], 0, 0)),
                pl.BlockSpec((2, win, win), lambda j, pattern, starts: (0, 0, 0)),
                pl.BlockSpec((2, win, win), lambda j, pattern, starts: (0, 0, 0)),
                pl.BlockSpec((1, 2, win, win), lambda j, pattern, starts: (lax.rem(j, 4), 0, 0, 0)),
            ],
            out_specs=[
                pl.BlockSpec((1, win, win), lambda j, pattern, starts: (j, 0, 0)),
                pl.BlockSpec((1, 2, win, win), lambda j, pattern, starts: (j, 0, 0, 0)),
                pl.BlockSpec((1, win, 3 * win), lambda j, pattern, starts: (j, 0, 0)),
                pl.BlockSpec((1, 3 * win, win), lambda j, pattern, starts: (j, 0, 0)),
            ],
        ),
        cost_estimate=pl.CostEstimate(flops=2 * 6 * positions * win**3, bytes_accessed=16 << 20, transcendentals=0),
        name="prepare",
    )(pattern, starts, measured, probe, order, parts)


def complex_mul(left_re, left_im, right_re, right_im):
    return (left_re * right_re - left_im * right_im, left_re * right_im + left_im * right_re)


def conj_mul(left_re, left_im, right_re, right_im):
    return (left_re * right_re + left_im * right_im, left_re * right_im - left_im * right_re)


def put_left(ref, side, row, value):
    high = value.astype(bf16)
    low = (value - high.astype(f32)).astype(bf16)
    size = value.shape[0]
    ref[side, row : row + size, :] = high
    ref[side, win + row : win + row + size, :] = low
    ref[side, 2 * win + row : 2 * win + row + size, :] = high


def put_right(ref, side, row, lane, value):
    high = value.astype(bf16)
    low = (value - high.astype(f32)).astype(bf16)
    size = value.shape[0]
    ref[side, row : row + size, lane : lane + half] = high
    ref[side, row : row + size, win + lane : win + lane + half] = low
    ref[side, row : row + size, 2 * win + lane : 2 * win + lane + half] = high


def core_body(
    starts_ref, flags_ref,
    one_ref, ca1_ref, cb1_ref, ra1_ref, rb1_ref, two_ref, ra2_ref, rb2_ref, ca2_ref, cb2_ref,
    rolled_ref, sorted_ref, ltab_ref, rtab_ref,
    wall_a, wall_b, mid_one, slab_a, slab_b, mid_two, out_keep, out_send,
    wide, total, share, *slots,
):
    step = pl.program_id(0)
    R = rows_at_once
    row_odd, col_odd = flags_ref[0], flags_ref[1]
    row_a = pl.multiple_of((1 - row_odd) * (win + half), half)
    row_b = pl.multiple_of(row_odd * (win + half), half)
    lane_a = pl.multiple_of((1 - col_odd) * (win + half), half)
    lane_b = pl.multiple_of(col_odd * (win + half), half)

    @pl.when(step == 0)
    def _():
        wide[0:2, pl.ds(row_a, half), :] = ra1_ref[...]
        wide[0:2, pl.ds(row_b, half), :] = rb1_ref[...]
        wide[0:2, half : half + win, pl.ds(lane_a, half)] = ca1_ref[...]
        wide[0:2, half : half + win, pl.ds(lane_b, half)] = cb1_ref[...]
        wide[0:2, half : half + win, half : half + win] = one_ref[...]
        wide[2:4, 0 : 2 * win, pl.ds(lane_a, half)] = ca2_ref[...]
        wide[2:4, 0 : 2 * win, pl.ds(lane_b, half)] = cb2_ref[...]
        wide[2:4, pl.ds(row_a, half), half : half + win] = ra2_ref[...]
        wide[2:4, pl.ds(row_b, half), half : half + win] = rb2_ref[...]
        wide[2:4, half : half + win, half : half + win] = two_ref[...]
        total[...] = jnp.zeros_like(total)
        share[...] = jnp.zeros_like(share)

    def work(slot):
        xa, xb, res, phi, shares = slots[5 * slot : 5 * slot + 5]
        position = at_once * step + slot
        a = starts_ref[position, 0]
        b = starts_ref[position, 1]
        offset = lax.rem(a, 8)
        base = pl.multiple_of(a - offset, 8)
        near = lax.broadcasted_iota(jnp.int32, (R, win), 1) >= b
        below = lax.broadcasted_iota(jnp.int32, (R, win), 0) >= offset

        def row_sets(row):
            first = (pl.ds(base + row, R), None)
            return (first,) if row else (first, (pl.ds(base + win, R), below))

        def window(plane, row):
            value = None
            for rows, mask in row_sets(row):
                block = jnp.where(near, wide[plane, rows, 0:win], wide[plane, rows, win : 2 * win])
                value = block if mask is None else jnp.where(mask, value, block)
            return value

        def add_window(plane, row, value):
            zero = jnp.zeros_like(value)
            for rows, mask in row_sets(row):
                part = value
                if row == 0:
                    part = jnp.where(below, value, zero) if mask is None else jnp.where(below, zero, value)
                total[plane, rows, 0:win] += jnp.where(near, part, zero)
                total[plane, rows, win : 2 * win] += jnp.where(near, zero, part)

        def left_stage(first):
            for side in range(2):
                res[side] = jnp.dot(ltab_ref[first + side], xa[side], preferred_element_type=f32)

        def right_stage(first):
            for side in range(2):
                res[side] = jnp.dot(xb[side], rtab_ref[first + side], preferred_element_type=f32)

        def row_butterfly(row, upper, lower):
            for part in range(2):
                put_left(xa, 0, part * half + row, upper[part] + lower[part])
                put_left(xa, 1, part * half + row, upper[part] - lower[part])

        def lane_butterfly(row, field):
            for part in range(2):
                near_half, far_half = field[part][:, :half], field[part][:, half:]
                put_right(xb, 0, row, part * half, near_half + far_half)
                put_right(xb, 1, row, part * half, near_half - far_half)

        def lane_join(row):
            out = []
            for part in range(2):
                plus = res[0, row : row + R, part * half : (part + 1) * half]
                minus = res[1, row : row + R, part * half : (part + 1) * half]
                out.append(jnp.concatenate([plus + minus, plus - minus], axis=1))
            return out

        def row_join(row):
            plus = [res[0, part * half + row : part * half + row + R, :] for part in range(2)]
            minus = [res[1, part * half + row : part * half + row + R, :] for part in range(2)]
            return [p + m for p, m in zip(plus, minus)], [p - m for p, m in zip(plus, minus)]

        def rows_to_lanes():
            for row in range(0, half, R):
                upper, lower = row_join(row)
                lane_butterfly(row, upper)
                lane_butterfly(half + row, lower)

        def add_share(plane, value):
            value = pltpu.roll(value, jnp.where(offset == 0, 0, win - offset), axis=0)
            share[plane] += pltpu.roll(value, jnp.where(b == 0, 0, win - b), axis=1)

        def probe(part, row):
            return rolled_ref[slot, part, row : row + R, :]

        for row in range(0, half, R):
            pair = []
            for at in (row, half + row):
                o_re, o_im = window(0, at), window(1, at)
                shares[0, at : at + R, :] = o_re * o_re + o_im * o_im
                pair.append(complex_mul(probe(0, at), probe(1, at), o_re, o_im))
            row_butterfly(row, *pair)
        yield
        left_stage(4)
        add_share(2, shares[0])
        yield
        rows_to_lanes()
        yield
        right_stage(0)
        yield
        for row in range(0, half, R):
            pair = []
            for at in (row, half + row):
                p_re, p_im = lane_join(at)
                phi[0, at : at + R, :] = p_re
                phi[1, at : at + R, :] = p_im
                pair.append(complex_mul(p_re, p_im, window(2, at), window(3, at)))
            row_butterfly(row, *pair)
        yield
        left_stage(6)
        yield
        for side in range(2):
            for row in range(0, half, R):
                lane_butterfly(
                    side * half + row, [res[side, part * half + row : part * half + row + R, :] for part in range(2)]
                )
        yield
        right_stage(2)
        yield
        for side in range(2):
            for row in range(0, win, R):
                far_re = res[side, row : row + R, 0:half]
                far_im = res[side, row : row + R, half:win]
                amplitude = sorted_ref[slot, row : row + R, side * half : (side + 1) * half]
                factor = 1.0 - amplitude * lax.rsqrt(far_re * far_re + far_im * far_im + 1.0)
                put_right(xb, side, row, 0, factor * far_re)
                put_right(xb, side, row, half, factor * far_im)
        yield
        right_stage(6)
        yield
        for side in range(2):
            for row in range(0, half, R):
                field = lane_join(side * half + row)
                for part in range(2):
                    put_left(xa, side, part * half + row, field[part])
        yield
        left_stage(2)
        yield
        for row in range(0, half, R):
            pair = []
            for at, (g_re, g_im) in zip((row, half + row), row_join(row)):
                t_re, t_im = conj_mul(phi[0, at : at + R, :], phi[1, at : at + R, :], g_re, g_im)
                add_window(2, at, t_re)
                add_window(3, at, t_im)
                pair.append(conj_mul(window(2, at), window(3, at), g_re, g_im))
            row_butterfly(row, *pair)
        yield
        left_stage(0)
        yield
        rows_to_lanes()
        yield
        right_stage(4)
        yield
        for at in range(0, win, R):
            g_re, g_im = lane_join(at)
            t_re, t_im = conj_mul(probe(0, at), probe(1, at), g_re, g_im)
            add_window(0, at, t_re)
            add_window(1, at, t_im)
            s_re, s_im = conj_mul(window(0, at), window(1, at), g_re, g_im)
            shares[0, at : at + R, :] = s_re
            shares[1, at : at + R, :] = s_im
        add_share(0, shares[0])
        add_share(1, shares[1])
        yield

    running = [work(slot) for slot in range(at_once)]
    live = []
    while running or live:
        if running:
            live.append(running.pop(0))
        live = [w for w in live if next(w, "end") is None]

    @pl.when(step == positions // at_once - 1)
    def _():
        wall_a[...] = total[0:2, 0 : 2 * win, pl.ds(lane_a, half)]
        wall_b[...] = total[0:2, 0 : 2 * win, pl.ds(lane_b, half)]
        mid_one[...] = total[0:2, 0 : 2 * win, half : half + win]
        slab_a[...] = total[2:4, pl.ds(row_a, half), :]
        slab_b[...] = total[2:4, pl.ds(row_b, half), :]
        mid_two[...] = total[2:4, half : half + win, :]
        out_keep[...] = share[:, pl.ds(pl.multiple_of(col_odd * half, half), half), :]
        out_send[...] = share[:, pl.ds(pl.multiple_of((1 - col_odd) * half, half), half), :]


def whole(*shape):
    return pl.BlockSpec(shape, lambda *ids: (0,) * len(shape))


def core(starts, flags, pieces, rolled, ordered, ltab, rtab):
    wall, slab, share = (2, 2 * win, half), (2, half, 2 * win), (3, half, win)
    shapes = (wall, wall, (2, 2 * win, win), slab, slab, (2, win, 2 * win), share, share)
    slot = [
        pltpu.VMEM((2, 3 * win, win), bf16),
        pltpu.VMEM((2, win, 3 * win), bf16),
        pltpu.VMEM((2, win, win), f32),
        pltpu.VMEM((2, win, win), f32),
        pltpu.VMEM((2, win, win), f32),
    ]
    return pl.pallas_call(
        core_body,
        out_shape=[jax.ShapeDtypeStruct(shape, f32) for shape in shapes],
        grid_spec=pltpu.PrefetchScalarGridSpec(
            num_scalar_prefetch=2,
            grid=(positions // at_once,),
            in_specs=[
                *(whole(*piece.shape) for piece in pieces),
                pl.BlockSpec((at_once, 2, win, win), lambda j, *prefetched: (j, 0, 0, 0)),
                pl.BlockSpec((at_once, win, win), lambda j, *prefetched: (j, 0, 0)),
                whole(8, win, 3 * win), whole(8, 3 * win, win),
            ],
            out_specs=[whole(*shape) for shape in shapes],
            scratch_shapes=[
                pltpu.VMEM((4, 2 * win + 8, 2 * win), f32),
                pltpu.VMEM((4, 2 * win + 8, 2 * win), f32),
                pltpu.VMEM((3, win, win), f32),
            ] + slot * at_once,
        ),
        compiler_params=pltpu.CompilerParams(vmem_limit_bytes=60 << 20),
        cost_estimate=pl.CostEstimate(flops=48 * 2 * positions * win**3, bytes_accessed=32 << 20, transcendentals=0),
        name="core",
    )(starts, flags, *pieces, rolled, ordered, ltab, rtab)


def small_kernel(kernel, name, flags, inputs, shapes):
    size = sum(x.size for x in inputs) + sum(math.prod(shape) for shape in shapes)
    return pl.pallas_call(
        kernel,
        out_shape=[jax.ShapeDtypeStruct(shape, f32) for shape in shapes],
        grid_spec=pltpu.PrefetchScalarGridSpec(
            num_scalar_prefetch=1,
            grid=(1,),
            in_specs=[whole(*x.shape) for x in inputs],
            out_specs=[whole(*shape) for shape in shapes],
        ),
        compiler_params=pltpu.CompilerParams(vmem_limit_bytes=48 << 20),
        cost_estimate=pl.CostEstimate(flops=size, bytes_accessed=4 * size, transcendentals=0),
        name=name,
    )(flags, *inputs)


def half_at(choice):
    return pl.ds(pl.multiple_of(choice * half, half), half)


def pack_first(flags_ref, one_ref, two_ref, ca_ref, cb_ref, ra_ref, rb_ref):
    row_odd, col_odd = flags_ref[0], flags_ref[1]
    for out, lanes in ((ca_ref, half_at(1 - col_odd)), (cb_ref, half_at(col_odd))):
        out[...] = one_ref[:, :, lanes]
    for out, rows in ((ra_ref, half_at(1 - row_odd)), (rb_ref, half_at(row_odd))):
        out[...] = two_ref[:, rows, :]


def pack_slabs(flags_ref, one_ref, ca_ref, cb_ref, a_ref, b_ref):
    row_odd, col_odd = flags_ref[0], flags_ref[1]
    for out, rows in ((a_ref, half_at(1 - row_odd)), (b_ref, half_at(row_odd))):
        out[:, :, half : half + win] = one_ref[:, rows, :]
        out[:, :, half_at(3 * (1 - col_odd))] = ca_ref[:, rows, :]
        out[:, :, half_at(3 * col_odd)] = cb_ref[:, rows, :]


def pack_walls(flags_ref, two_ref, ra_ref, rb_ref, a_ref, b_ref):
    row_odd, col_odd = flags_ref[0], flags_ref[1]
    for out, lanes in ((a_ref, half_at(1 - col_odd)), (b_ref, half_at(col_odd))):
        out[:, half : half + win, :] = two_ref[:, :, lanes]
        out[:, half_at(3 * (1 - row_odd)), :] = ra_ref[:, :, lanes]
        out[:, half_at(3 * row_odd), :] = rb_ref[:, :, lanes]


def fold_slabs(flags_ref, mid_ref, qa_ref, qb_ref, a_ref, b_ref, center_ref):
    row_odd, col_odd = flags_ref[0], flags_ref[1]
    for got, rows in ((qa_ref, half_at(1 - row_odd)), (qb_ref, half_at(row_odd))):
        center_ref[:, rows, :] = mid_ref[:, rows, half : half + win] + got[:, :, half : half + win]
        for out, lanes in ((a_ref, half_at(3 * (1 - col_odd))), (b_ref, half_at(3 * col_odd))):
            out[:, rows, :] = mid_ref[:, rows, lanes] + got[:, :, lanes]


def fold_walls(flags_ref, mid_ref, qa_ref, qb_ref, a_ref, b_ref, center_ref):
    row_odd, col_odd = flags_ref[0], flags_ref[1]
    for got, lanes in ((qa_ref, half_at(1 - col_odd)), (qb_ref, half_at(col_odd))):
        center_ref[:, :, lanes] = mid_ref[:, half : half + win, lanes] + got[:, half : half + win, :]
        for out, rows in ((a_ref, half_at(3 * (1 - row_odd))), (b_ref, half_at(3 * row_odd))):
            out[:, :, lanes] = mid_ref[:, rows, lanes] + got[:, rows, :]


def fold_columns(flags_ref, center_ref, a_ref, b_ref, out_ref):
    odd = flags_ref[1]
    for got, lanes in ((a_ref, half_at(1 - odd)), (b_ref, half_at(odd))):
        out_ref[:, :, lanes] = center_ref[:, :, lanes] + got[...]


def fold_rows(flags_ref, center_ref, a_ref, b_ref, out_ref):
    odd = flags_ref[0]
    for got, rows in ((a_ref, half_at(1 - odd)), (b_ref, half_at(odd))):
        out_ref[:, rows, :] = center_ref[:, rows, :] + got[...]


def pack_share(flags_ref, keep_ref, got_ref, out_ref):
    for tile in range(64):
        for plane, spot in ((tile // 32, 0), (2, 8)):
            rows = slice(tile % 32 // 2 * 8, tile % 32 // 2 * 8 + 8)
            lanes = slice(tile % 2 * half, tile % 2 * half + half)
            out_ref[tile, spot : spot + 8, :] = keep_ref[plane, rows, lanes] + got_ref[plane, rows, lanes]


def take_step(flags_ref, parts_ref, out_ref):
    total = parts_ref[0]
    for tile in range(1, 64):
        total = total + parts_ref[tile]
    step = total[0:8] * lax.rsqrt(total[8:16] + 1.0)
    for tile in range(64):
        out_ref[tile] = step


def join_step(flags_ref, own_ref, other_ref, out_ref):
    odd = flags_ref[1]
    for tile in range(64):
        row = tile % 32 // 2 * 8
        lanes = slice(tile % 2 * half, tile % 2 * half + half)
        out_ref[tile // 32, pl.ds(pl.multiple_of(odd * half + row, 8), 8), lanes] = own_ref[tile]
        out_ref[tile // 32, pl.ds(pl.multiple_of((1 - odd) * half + row, 8), 8), lanes] = other_ref[tile]


def swapped(block, axis, first):
    pairs = [(i, i + 1) for i in range(first, lax.axis_size(axis) - 1, 2)]
    return lax.ppermute(block, axis, pairs + [(j, i) for i, j in pairs])


def exchanged(parts):
    rows, cols = lax.axis_size("row"), lax.axis_size("col")
    groups = [[r * cols + c for r in range(rows) for c in range(odd, cols, 2)] for odd in range(2)]
    return lax.all_to_all(parts, ("row", "col"), 0, 0, axis_index_groups=groups, tiled=True)


def body(object_one, object_two, probe, scan_pos, pattern_index, measured):
    starts = scan_pos[0, 0]
    flags = jnp.stack([lax.axis_index("row") % 2, lax.axis_index("col") % 2]).astype(jnp.int32)
    side, edge, wall, slab, tile = (2, win, half), (2, half, win), (2, 2 * win, half), (2, half, 2 * win), (2, win, win)
    first = small_kernel(pack_first, "pack_first", flags, (object_one, object_two), (side, side, edge, edge))
    ca1, cb1 = swapped(first[0], "col", 0), swapped(first[1], "col", 1)
    ra2, rb2 = swapped(first[2], "row", 0), swapped(first[3], "row", 1)
    ra1, rb1 = small_kernel(pack_slabs, "pack_slabs", flags, (object_one, ca1, cb1), (slab, slab))
    ra1, rb1 = swapped(ra1, "row", 0), swapped(rb1, "row", 1)
    ca2, cb2 = small_kernel(pack_walls, "pack_walls", flags, (object_two, ra2, rb2), (wall, wall))
    ca2, cb2 = swapped(ca2, "col", 0), swapped(cb2, "col", 1)
    ordered, rolled, ltab, rtab = prepare(pattern_index[0, 0], starts, measured[0, 0], probe)
    pieces = (object_one, ca1, cb1, ra1, rb1, object_two, ra2, rb2, ca2, cb2)
    wa, wb, mid_one, sa, sb, mid_two, keep, send = core(starts, flags, pieces, rolled, ordered, ltab, rtab)
    share = small_kernel(pack_share, "pack_share", flags, (keep, swapped(send, "col", 0)), ((64, 16, half),))[0]
    sa, sb = swapped(sa, "row", 0), swapped(sb, "row", 1)
    wa, wb = swapped(wa, "col", 0), swapped(wb, "col", 1)
    ga, gb, center_one = small_kernel(fold_walls, "fold_walls", flags, (mid_one, wa, wb), (edge, edge, tile))
    ga, gb = swapped(ga, "row", 0), swapped(gb, "row", 1)
    ha, hb, center_two = small_kernel(fold_slabs, "fold_slabs", flags, (mid_two, sa, sb), (side, side, tile))
    ha, hb = swapped(ha, "col", 0), swapped(hb, "col", 1)
    step = small_kernel(take_step, "take_step", flags, (exchanged(share),), ((64, 8, half),))[0]
    step = exchanged(step)
    grad_one = small_kernel(fold_rows, "fold_rows", flags, (center_one, ga, gb), (tile,))[0]
    grad_two = small_kernel(fold_columns, "fold_columns", flags, (center_two, ha, hb), (tile,))[0]
    probe_step = small_kernel(join_step, "join_step", flags, (step, swapped(step, "col", 0)), (tile,))[0]
    return (grad_one, grad_two, probe_step)


def solution(mesh):
    placed = (
        P(None, "row", "col"),
        P(None, "row", "col"),
        P(),
        P("row", "col", None, None),
        P("row", "col", None),
        P("row", "col", None, None, None),
    )
    return jax.shard_map(
        body,
        mesh=mesh,
        in_specs=placed,
        out_specs=(P(None, "row", "col"), P(None, "row", "col"), P()),
        check_vma=False,
    )
```

```python
import math

import jax
import jax.numpy as jnp
import ml_dtypes
import numpy as np
from jax import lax
from jax.experimental import pallas as pl
from jax.experimental.pallas import tpu as pltpu
from jax.sharding import PartitionSpec as P

phase_rate = 0.002
win = 256
half = 128
positions = 8
R = 16
at_once = 2
f32 = jnp.float32
bf16 = jnp.bfloat16


def real_form(table):
    return np.block([[table.real, table.imag], [-table.imag, table.real]])


def split_table(table):
    high = table.astype(np.float32).astype(ml_dtypes.bfloat16)
    low = (table - high.astype(np.float64)).astype(ml_dtypes.bfloat16)
    return high, low


def factor_tables():
    counter = np.arange(win)
    frequency = np.where(counter < half, counter, counter - win)
    kernel = np.exp(-1j * phase_rate * frequency.astype(np.float64) ** 2)
    response = np.fft.ifft(kernel)
    circulant = response[(counter[:, None] - counter[None, :]) % win]
    first, second = circulant[:half, :half], circulant[:half, half:]
    n, k = np.arange(half)[:, None], np.arange(half)[None, :]
    even = np.exp(-2j * np.pi * ((2 * n * k) % win) / win) / 16.0
    odd = np.exp(-2j * np.pi * ((n * (2 * k + 1)) % win) / win) / 16.0
    return [real_form(t) for t in (0.5 * (first + second), 0.5 * (first - second), even, odd)]


def table_parts():
    factors = factor_tables()
    return np.stack([np.stack(split_table(table)) for table in factors + [t.T for t in factors]])


def column_order():
    order = np.concatenate([np.arange(0, win, 2), np.arange(1, win, 2)])
    table = np.zeros((win, win), np.float32)
    table[order, np.arange(win)] = 1.0
    return table.astype(ml_dtypes.bfloat16)


def split3(value):
    high = value.astype(bf16)
    rest = value - high.astype(f32)
    middle = rest.astype(bf16)
    low = (rest - middle.astype(f32)).astype(bf16)
    return high, middle, low


steps_before = 2


def sort_body(pattern_ref, near_ref, far_ref, order_ref, sorted_ref):
    order = order_ref[...]
    many = positions // steps_before

    def one_position(spot, carry):
        pattern = pattern_ref[pl.program_id(0) * many + spot]
        for parity in range(2):
            rows = [ref[pattern, pl.ds(parity, half, stride=2), :] for ref in (near_ref, far_ref)]
            parts = split3(jnp.concatenate(rows, axis=1))
            sorted_ref[spot, parity * half : (parity + 1) * half, :] = sum(
                jnp.dot(part, order, preferred_element_type=f32) for part in parts
            )
        return carry

    lax.fori_loop(0, many, one_position, 0)


def sort_patterns(pattern, measured):
    return pl.pallas_call(
        sort_body,
        out_shape=jax.ShapeDtypeStruct((positions, win, win), f32),
        grid_spec=pltpu.PrefetchScalarGridSpec(
            num_scalar_prefetch=1,
            grid=(steps_before,),
            in_specs=[
                pl.BlockSpec((positions, win, half), lambda j, pattern: (0, 0, 0)),
                pl.BlockSpec((positions, win, half), lambda j, pattern: (0, 0, 1)),
                whole(win, win),
            ],
            out_specs=pl.BlockSpec((positions // steps_before, win, win), lambda j, pattern: (j, 0, 0)),
        ),
        cost_estimate=pl.CostEstimate(flops=2 * 3 * positions * win**3, bytes_accessed=4 << 20, transcendentals=0),
        name="sort_patterns",
    )(pattern, measured, measured, jnp.asarray(column_order()))


def prepare_body(starts_ref, probe_ref, parts_ref, rolled_ref, left_ref, right_ref):
    many = positions // steps_before

    def one_position(spot, carry):
        position = pl.program_id(0) * many + spot
        down = lax.rem(starts_ref[position, 0], 8)
        across = starts_ref[position, 1]
        kept = lax.broadcasted_iota(jnp.int32, (8, win), 0) >= down
        for plane in range(2):
            above = pltpu.roll(probe_ref[plane, win - 8 : win, :], down, axis=0)
            for row in range(0, win, 8):
                block = pltpu.roll(probe_ref[plane, row : row + 8, :], down, axis=0)
                rolled_ref[spot, plane, row : row + 8, :] = pltpu.roll(jnp.where(kept, block, above), across, axis=1)
                above = block
        for part, places in ((0, (0, 1)), (1, (2,))):
            table = parts_ref[spot, part]
            for place in places:
                left_ref[spot, :, place * win : (place + 1) * win] = table
                right_ref[spot, place * win : (place + 1) * win, :] = table
        return carry

    lax.fori_loop(0, many, one_position, 0)


def prepare(starts, probe):
    many = positions // steps_before
    return pl.pallas_call(
        prepare_body,
        out_shape=(
            jax.ShapeDtypeStruct((positions, 2, win, win), f32),
            jax.ShapeDtypeStruct((8, win, 3 * win), bf16),
            jax.ShapeDtypeStruct((8, 3 * win, win), bf16),
        ),
        grid_spec=pltpu.PrefetchScalarGridSpec(
            num_scalar_prefetch=1,
            grid=(steps_before,),
            in_specs=[
                whole(2, win, win),
                pl.BlockSpec((many, 2, win, win), lambda j, starts: (j, 0, 0, 0)),
            ],
            out_specs=[
                pl.BlockSpec((many, 2, win, win), lambda j, starts: (j, 0, 0, 0)),
                pl.BlockSpec((many, win, 3 * win), lambda j, starts: (j, 0, 0)),
                pl.BlockSpec((many, 3 * win, win), lambda j, starts: (j, 0, 0)),
            ],
        ),
        compiler_params=pltpu.CompilerParams(vmem_limit_bytes=44 << 20),
        cost_estimate=pl.CostEstimate(flops=positions * win**3, bytes_accessed=12 << 20, transcendentals=0),
        name="prepare",
    )(starts, probe, jnp.asarray(table_parts()))


def complex_mul(left_re, left_im, right_re, right_im):
    return (left_re * right_re - left_im * right_im, left_re * right_im + left_im * right_re)


def conj_mul(left_re, left_im, right_re, right_im):
    return (left_re * right_re + left_im * right_im, left_re * right_im - left_im * right_re)


def put_left(ref, side, row, value):
    high = value.astype(bf16)
    low = (value - high.astype(f32)).astype(bf16)
    size = value.shape[0]
    ref[side, row : row + size, :] = high
    ref[side, win + row : win + row + size, :] = low
    ref[side, 2 * win + row : 2 * win + row + size, :] = high


def put_right(ref, side, row, lane, value):
    high = value.astype(bf16)
    low = (value - high.astype(f32)).astype(bf16)
    size = value.shape[0]
    ref[side, row : row + size, lane : lane + half] = high
    ref[side, row : row + size, win + lane : win + lane + half] = low
    ref[side, row : row + size, 2 * win + lane : 2 * win + lane + half] = high


class Work:
    def __init__(self, starts_ref, position, wide, total, xa, xb, res):
        self.wide, self.total, self.xa, self.xb, self.res = wide, total, xa, xb, res
        a = starts_ref[position, 0]
        self.b = starts_ref[position, 1]
        self.offset = lax.rem(a, 8)
        self.base = pl.multiple_of(a - self.offset, 8)
        self.near = lax.broadcasted_iota(jnp.int32, (R, win), 1) >= self.b
        self.below = lax.broadcasted_iota(jnp.int32, (R, win), 0) >= self.offset

    def row_sets(self, row):
        first = (pl.ds(self.base + row, R), None)
        return (first,) if row else (first, (pl.ds(self.base + win, R), self.below))

    def window(self, plane, row):
        value = None
        for rows, mask in self.row_sets(row):
            block = jnp.where(self.near, self.wide[plane, rows, 0:win], self.wide[plane, rows, win : 2 * win])
            value = block if mask is None else jnp.where(mask, value, block)
        return value

    def add_window(self, plane, row, value):
        zero = jnp.zeros_like(value)
        for rows, mask in self.row_sets(row):
            part = value
            if row == 0:
                part = jnp.where(self.below, value, zero) if mask is None else jnp.where(self.below, zero, value)
            self.total[plane, rows, 0:win] += jnp.where(self.near, part, zero)
            self.total[plane, rows, win : 2 * win] += jnp.where(self.near, zero, part)

    def left_stage(self, table):
        for side in range(2):
            self.res[side] = jnp.dot(table[side], self.xa[side], preferred_element_type=f32)

    def right_stage(self, table):
        for side in range(2):
            self.res[side] = jnp.dot(self.xb[side], table[side], preferred_element_type=f32)

    def row_butterfly(self, row, upper, lower):
        for part in range(2):
            put_left(self.xa, 0, part * half + row, upper[part] + lower[part])
            put_left(self.xa, 1, part * half + row, upper[part] - lower[part])

    def lane_butterfly(self, row, field):
        for part in range(2):
            near_half, far_half = field[part][:, :half], field[part][:, half:]
            put_right(self.xb, 0, row, part * half, near_half + far_half)
            put_right(self.xb, 1, row, part * half, near_half - far_half)

    def lane_join(self, row):
        out = []
        for part in range(2):
            plus = self.res[0, row : row + R, part * half : (part + 1) * half]
            minus = self.res[1, row : row + R, part * half : (part + 1) * half]
            out.append(jnp.concatenate([plus + minus, plus - minus], axis=1))
        return out

    def row_join(self, row):
        plus = [self.res[0, part * half + row : part * half + row + R, :] for part in range(2)]
        minus = [self.res[1, part * half + row : part * half + row + R, :] for part in range(2)]
        return [p + m for p, m in zip(plus, minus)], [p - m for p, m in zip(plus, minus)]

    def rows_to_lanes(self):
        for row in range(0, half, R):
            upper, lower = self.row_join(row)
            self.lane_butterfly(row, upper)
            self.lane_butterfly(half + row, lower)

    def add_unrolled(self, target, source):
        up = jnp.where(self.offset == 0, 0, 8 - self.offset)
        across = jnp.where(self.b == 0, 0, win - self.b)
        kept = lax.broadcasted_iota(jnp.int32, (8, win), 0) < 8 - self.offset
        first = block = pltpu.roll(source[0:8, :], up, axis=0)
        for row in range(0, win, 8):
            below = pltpu.roll(source[row + 8 : row + 16, :], up, axis=0) if row + 8 < win else first
            target[row : row + 8, :] += pltpu.roll(jnp.where(kept, block, below), across, axis=1)
            block = below


def run_together(works):
    running, live = list(works), []
    while running or live:
        if running:
            live.append(running.pop(0))
        live = [w for w in live if next(w, "end") is None]


def assemble(flags_ref, wide, own_ref, ra_ref, rb_ref, ca_ref, cb_ref):
    row_odd, col_odd = flags_ref[0], flags_ref[1]
    wide[:, half_at(3 * (1 - row_odd)), half : half + win] = ra_ref[...]
    wide[:, half_at(3 * row_odd), half : half + win] = rb_ref[...]
    wide[:, 0 : 2 * win, half_at(3 * (1 - col_odd))] = ca_ref[...]
    wide[:, 0 : 2 * win, half_at(3 * col_odd)] = cb_ref[...]
    wide[:, half : half + win, half : half + win] = own_ref[...]


def give_out(flags_ref, total, wall_a, wall_b, mid):
    col_odd = flags_ref[1]
    wall_a[...] = total[:, 0 : 2 * win, half_at(3 * (1 - col_odd))]
    wall_b[...] = total[:, 0 : 2 * win, half_at(3 * col_odd)]
    mid[...] = total[:, 0 : 2 * win, half : half + win]


def propagate_body(
    starts_ref, flags_ref, own_ref, ra_ref, rb_ref, ca_ref, cb_ref, rolled_ref, left_ref, right_ref,
    phi_ref, wide, light, *slots,
):
    step = pl.program_id(0)

    @pl.when(step == 0)
    def _():
        assemble(flags_ref, wide, own_ref, ra_ref, rb_ref, ca_ref, cb_ref)
        light[...] = jnp.zeros_like(light)

    def work(slot):
        xa, xb, res, shares = slots[4 * slot : 4 * slot + 4]
        w = Work(starts_ref, at_once * step + slot, wide, None, xa, xb, res)
        for row in range(0, half, R):
            pair = []
            for at in (row, half + row):
                o_re, o_im = w.window(0, at), w.window(1, at)
                shares[0, at : at + R, :] = o_re * o_re + o_im * o_im
                probe = [rolled_ref[slot, part, at : at + R, :] for part in range(2)]
                pair.append(complex_mul(*probe, o_re, o_im))
            w.row_butterfly(row, *pair)
        yield
        w.left_stage(left_ref)
        w.add_unrolled(light, shares.at[0])
        yield
        w.rows_to_lanes()
        yield
        w.right_stage(right_ref)
        yield
        for row in range(0, win, R):
            phi_ref[slot, 0, row : row + R, :], phi_ref[slot, 1, row : row + R, :] = w.lane_join(row)
        yield

    run_together(work(slot) for slot in range(at_once))


def detect_body(
    starts_ref, flags_ref, own_ref, ra_ref, rb_ref, ca_ref, cb_ref, phi_ref, sorted_ref,
    left_ref, right_ref, left_back, right_back,
    inner_ref, wall_a, wall_b, mid, wide, total, *slots,
):
    step = pl.program_id(0)

    @pl.when(step == 0)
    def _():
        assemble(flags_ref, wide, own_ref, ra_ref, rb_ref, ca_ref, cb_ref)
        total[...] = jnp.zeros_like(total)

    def work(slot):
        xa, xb, res = slots[4 * slot : 4 * slot + 3]
        w = Work(starts_ref, at_once * step + slot, wide, total, xa, xb, res)

        def phi(row):
            return [phi_ref[slot, part, row : row + R, :] for part in range(2)]

        for row in range(0, half, R):
            pair = [complex_mul(*phi(at), w.window(0, at), w.window(1, at)) for at in (row, half + row)]
            w.row_butterfly(row, *pair)
        yield
        w.left_stage(left_ref)
        yield
        for side in range(2):
            for row in range(0, half, R):
                w.lane_butterfly(
                    side * half + row, [res[side, part * half + row : part * half + row + R, :] for part in range(2)]
                )
        yield
        w.right_stage(right_ref)
        yield
        for side in range(2):
            for row in range(0, win, R):
                far_re = res[side, row : row + R, 0:half]
                far_im = res[side, row : row + R, half:win]
                amplitude = sorted_ref[slot, row : row + R, side * half : (side + 1) * half]
                factor = 1.0 - amplitude * lax.rsqrt(far_re * far_re + far_im * far_im + 1.0)
                put_right(xb, side, row, 0, factor * far_re)
                put_right(xb, side, row, half, factor * far_im)
        yield
        w.right_stage(right_back)
        yield
        for side in range(2):
            for row in range(0, half, R):
                field = w.lane_join(side * half + row)
                for part in range(2):
                    put_left(xa, side, part * half + row, field[part])
        yield
        w.left_stage(left_back)
        yield
        for row in range(0, half, R):
            for at, back in zip((row, half + row), w.row_join(row)):
                for part, term in enumerate(conj_mul(*phi(at), *back)):
                    w.add_window(part, at, term)
                inner = conj_mul(w.window(0, at), w.window(1, at), *back)
                inner_ref[slot, 0, at : at + R, :], inner_ref[slot, 1, at : at + R, :] = inner
        yield

    run_together(work(slot) for slot in range(at_once))

    @pl.when(step == positions // at_once - 1)
    def _():
        give_out(flags_ref, total, wall_a, wall_b, mid)


def return_body(
    starts_ref, flags_ref, wide, inner_ref, rolled_ref, light, left_ref, right_ref,
    wall_a, wall_b, mid, keep, send, total, share, *slots,
):
    step = pl.program_id(0)

    @pl.when(step == 0)
    def _():
        total[...] = jnp.zeros_like(total)
        share[0:2] = jnp.zeros((2, win, win), f32)
        share[2] = light[...]

    def work(slot):
        xa, xb, res, shares = slots[4 * slot : 4 * slot + 4]
        w = Work(starts_ref, at_once * step + slot, wide, total, xa, xb, res)
        for row in range(0, half, R):
            pair = [[inner_ref[slot, part, at : at + R, :] for part in range(2)] for at in (row, half + row)]
            w.row_butterfly(row, *pair)
        yield
        w.left_stage(left_ref)
        yield
        w.rows_to_lanes()
        yield
        w.right_stage(right_ref)
        yield
        for at in range(0, win, R):
            entry = w.lane_join(at)
            probe = [rolled_ref[slot, part, at : at + R, :] for part in range(2)]
            for part, term in enumerate(conj_mul(*probe, *entry)):
                w.add_window(part, at, term)
            terms = conj_mul(w.window(0, at), w.window(1, at), *entry)
            shares[0, at : at + R, :], shares[1, at : at + R, :] = terms
        for part in range(2):
            w.add_unrolled(share.at[part], shares.at[part])
        yield

    run_together(work(slot) for slot in range(at_once))

    @pl.when(step == positions // at_once - 1)
    def _():
        give_out(flags_ref, total, wall_a, wall_b, mid)
        keep[...] = share[:, half_at(flags_ref[1]), :]
        send[...] = share[:, half_at(1 - flags_ref[1]), :]


def position_kernel(body, products, starts, flags, inputs, outputs, scratch):
    def spec(shape, kind):
        if kind == "each":
            return pl.BlockSpec((at_once,) + shape[1:], lambda j, *_: (j,) + (0,) * (len(shape) - 1))
        if kind == "whole":
            return whole(*shape)
        return pl.BlockSpec((2,) + shape[1:], lambda j, *_: (kind,) + (0,) * (len(shape) - 1))

    slot = [
        pltpu.VMEM((2, 3 * win, win), bf16),
        pltpu.VMEM((2, win, 3 * win), bf16),
        pltpu.VMEM((2, win, win), f32),
        pltpu.VMEM((2, win, win), f32),
    ]
    return pl.pallas_call(
        body,
        out_shape=[jax.ShapeDtypeStruct(shape, f32) for shape, _ in outputs],
        grid_spec=pltpu.PrefetchScalarGridSpec(
            num_scalar_prefetch=2,
            grid=(positions // at_once,),
            in_specs=[spec(x.shape, kind) for x, kind in inputs],
            out_specs=[spec(shape, kind) for shape, kind in outputs],
            scratch_shapes=scratch + slot * at_once,
        ),
        compiler_params=pltpu.CompilerParams(vmem_limit_bytes=44 << 20),
        cost_estimate=pl.CostEstimate(
            flops=products * 24 * positions * win**3, bytes_accessed=products * (8 << 20), transcendentals=0
        ),
    )(starts, flags, *(x for x, _ in inputs))


def whole(*shape):
    return pl.BlockSpec(shape, lambda *ids: (0,) * len(shape))


def small_kernel(kernel, flags, inputs, shapes):
    size = sum(x.size for x in inputs) + sum(math.prod(shape) for shape in shapes)
    return pl.pallas_call(
        kernel,
        out_shape=[jax.ShapeDtypeStruct(shape, f32) for shape in shapes],
        grid_spec=pltpu.PrefetchScalarGridSpec(
            num_scalar_prefetch=1,
            grid=(1,),
            in_specs=[whole(*x.shape) for x in inputs],
            out_specs=[whole(*shape) for shape in shapes],
        ),
        compiler_params=pltpu.CompilerParams(vmem_limit_bytes=48 << 20),
        cost_estimate=pl.CostEstimate(flops=size, bytes_accessed=4 * size, transcendentals=0),
    )(flags, *inputs)


def half_at(choice):
    return pl.ds(pl.multiple_of(choice * half, half), half)


def pack_edges(flags_ref, own_ref, a_ref, b_ref):
    row_odd = flags_ref[0]
    for out, rows in ((a_ref, half_at(1 - row_odd)), (b_ref, half_at(row_odd))):
        out[...] = own_ref[:, rows, :]


def pack_walls(flags_ref, two_ref, ra_ref, rb_ref, a_ref, b_ref):
    row_odd, col_odd = flags_ref[0], flags_ref[1]
    for out, lanes in ((a_ref, half_at(1 - col_odd)), (b_ref, half_at(col_odd))):
        out[:, half : half + win, :] = two_ref[:, :, lanes]
        out[:, half_at(3 * (1 - row_odd)), :] = ra_ref[:, :, lanes]
        out[:, half_at(3 * row_odd), :] = rb_ref[:, :, lanes]


def fold_walls(flags_ref, mid_ref, qa_ref, qb_ref, a_ref, b_ref, center_ref):
    row_odd, col_odd = flags_ref[0], flags_ref[1]
    for got, lanes in ((qa_ref, half_at(1 - col_odd)), (qb_ref, half_at(col_odd))):
        center_ref[:, :, lanes] = mid_ref[:, half : half + win, lanes] + got[:, half : half + win, :]
        for out, rows in ((a_ref, half_at(3 * (1 - row_odd))), (b_ref, half_at(3 * row_odd))):
            out[:, :, lanes] = mid_ref[:, rows, lanes] + got[:, rows, :]


def fold_rows(flags_ref, center_ref, a_ref, b_ref, out_ref):
    odd = flags_ref[0]
    for got, rows in ((a_ref, half_at(1 - odd)), (b_ref, half_at(odd))):
        out_ref[:, rows, :] = center_ref[:, rows, :] + got[...]


def pack_share(flags_ref, keep_ref, got_ref, out_ref):
    for tile in range(64):
        for plane, spot in ((tile // 32, 0), (2, 8)):
            rows = slice(tile % 32 // 2 * 8, tile % 32 // 2 * 8 + 8)
            lanes = slice(tile % 2 * half, tile % 2 * half + half)
            out_ref[tile, spot : spot + 8, :] = keep_ref[plane, rows, lanes] + got_ref[plane, rows, lanes]


def take_step(flags_ref, parts_ref, out_ref):
    total = parts_ref[0]
    for tile in range(1, 64):
        total = total + parts_ref[tile]
    step = total[0:8] * lax.rsqrt(total[8:16] + 1.0)
    for tile in range(64):
        out_ref[tile] = step


def join_step(flags_ref, own_ref, other_ref, out_ref):
    odd = flags_ref[1]
    for tile in range(64):
        row = tile % 32 // 2 * 8
        lanes = slice(tile % 2 * half, tile % 2 * half + half)
        out_ref[tile // 32, pl.ds(pl.multiple_of(odd * half + row, 8), 8), lanes] = own_ref[tile]
        out_ref[tile // 32, pl.ds(pl.multiple_of((1 - odd) * half + row, 8), 8), lanes] = other_ref[tile]


def swapped(block, axis, first):
    pairs = [(i, i + 1) for i in range(first, lax.axis_size(axis) - 1, 2)]
    return lax.ppermute(block, axis, pairs + [(j, i) for i, j in pairs])


def exchanged(parts):
    rows, cols = lax.axis_size("row"), lax.axis_size("col")
    groups = [[r * cols + c for r in range(rows) for c in range(odd, cols, 2)] for odd in range(2)]
    return lax.all_to_all(parts, ("row", "col"), 0, 0, axis_index_groups=groups, tiled=True)


def gradients(object_one, object_two, probe, scan_pos, pattern_index, measured):
    starts = scan_pos[0, 0]
    flags = jnp.stack([lax.axis_index("row") % 2, lax.axis_index("col") % 2]).astype(jnp.int32)
    edge, wall, tile = (2, half, win), (2, 2 * win, half), (2, win, win)

    def edges_of(own):
        ra, rb = small_kernel(pack_edges, flags, (own,), (edge, edge))
        return swapped(ra, "row", 0), swapped(rb, "row", 1)

    def walls_of(own, edges):
        ca, cb = small_kernel(pack_walls, flags, (own,) + edges, (wall, wall))
        return swapped(ca, "col", 0), swapped(cb, "col", 1)

    def folded(wa, wb, mid):
        wa = swapped(wa, "col", 0)
        wb = swapped(wb, "col", 1)
        ga, gb, center = small_kernel(fold_walls, flags, (mid, wa, wb), (edge, edge, tile))
        ga = swapped(ga, "row", 0)
        gb = swapped(gb, "row", 1)
        return small_kernel(fold_rows, flags, (center, ga, gb), (tile,))[0]

    edges_one, edges_two = edges_of(object_one), edges_of(object_two)
    walls_one = walls_of(object_one, edges_one)
    walls_two = walls_of(object_two, edges_two)
    ordered = sort_patterns(pattern_index[0, 0], measured[0, 0])
    rolled, ltab, rtab = prepare(starts, probe)
    stack, wide_shape = (positions, 2, win, win), (2, 2 * win + 8, 2 * win)
    parts = (wall, "whole"), (wall, "whole"), ((2, 2 * win, win), "whole")
    pieces = [(x, "whole") for x in (object_one,) + edges_one + walls_one]
    phi, wide, light = position_kernel(
        propagate_body, 1, starts, flags,
        pieces + [(rolled, "each"), (ltab, 2), (rtab, 0)],
        [(stack, "each"), (wide_shape, "whole"), ((win, win), "whole")], [],
    )
    pieces = [(x, "whole") for x in (object_two,) + edges_two + walls_two]
    inner, *two = position_kernel(
        detect_body, 2, starts, flags,
        pieces + [(phi, "each"), (ordered, "each"), (ltab, 3), (rtab, 1), (ltab, 1), (rtab, 3)],
        [(stack, "each"), *parts], [pltpu.VMEM(wide_shape, f32), pltpu.VMEM(wide_shape, f32)],
    )
    *one, keep, send = position_kernel(
        return_body, 1, starts, flags,
        [(wide, "whole"), (inner, "each"), (rolled, "each"), (light, "whole"), (ltab, 0), (rtab, 2)],
        [*parts, ((3, half, win), "whole"), ((3, half, win), "whole")],
        [pltpu.VMEM(wide_shape, f32), pltpu.VMEM((3, win, win), f32)],
    )
    share = small_kernel(pack_share, flags, (keep, swapped(send, "col", 0)), ((64, 16, half),))[0]
    grad_two = folded(*two)
    grad_one = folded(*one)
    step = small_kernel(take_step, flags, (exchanged(share),), ((64, 8, half),))[0]
    step = exchanged(step)
    probe_step = small_kernel(join_step, flags, (step, swapped(step, "col", 0)), (tile,))[0]
    return (grad_one, grad_two, probe_step)


def solution(mesh):
    placed = (
        P(None, "row", "col"),
        P(None, "row", "col"),
        P(),
        P("row", "col", None, None),
        P("row", "col", None),
        P("row", "col", None, None, None),
    )
    return jax.shard_map(
        gradients,
        mesh=mesh,
        in_specs=placed,
        out_specs=(P(None, "row", "col"), P(None, "row", "col"), P()),
        check_vma=False,
    )
```

```python
import math

import jax
import jax.numpy as jnp
import ml_dtypes
import numpy as np
from jax import lax
from jax.experimental import pallas as pl
from jax.experimental.pallas import tpu as pltpu
from jax.sharding import PartitionSpec as P

phase_rate = 0.002
win = 256
half = 128
positions = 8
R = 16
at_once = 2
f32 = jnp.float32
bf16 = jnp.bfloat16


def real_form(table):
    return np.block([[table.real, table.imag], [-table.imag, table.real]])


def split_table(table):
    high = table.astype(np.float32).astype(ml_dtypes.bfloat16)
    low = (table - high.astype(np.float64)).astype(ml_dtypes.bfloat16)
    return high, low


def factor_tables():
    counter = np.arange(win)
    frequency = np.where(counter < half, counter, counter - win)
    kernel = np.exp(-1j * phase_rate * frequency.astype(np.float64) ** 2)
    response = np.fft.ifft(kernel)
    circulant = response[(counter[:, None] - counter[None, :]) % win]
    first, second = circulant[:half, :half], circulant[:half, half:]
    n, k = np.arange(half)[:, None], np.arange(half)[None, :]
    even = np.exp(-2j * np.pi * ((2 * n * k) % win) / win) / 16.0
    odd = np.exp(-2j * np.pi * ((n * (2 * k + 1)) % win) / win) / 16.0
    return [real_form(t) for t in (0.5 * (first + second), 0.5 * (first - second), even, odd)]


def table_parts():
    factors = factor_tables()
    return np.stack([np.stack(split_table(table)) for table in factors + [t.T for t in factors]])


def column_order():
    order = np.concatenate([np.arange(0, win, 2), np.arange(1, win, 2)])
    table = np.zeros((win, win), np.float32)
    table[order, np.arange(win)] = 1.0
    return table.astype(ml_dtypes.bfloat16)


def split3(value):
    high = value.astype(bf16)
    rest = value - high.astype(f32)
    middle = rest.astype(bf16)
    low = (rest - middle.astype(f32)).astype(bf16)
    return high, middle, low


steps_before = 2


def sort_body(pattern_ref, near_ref, far_ref, order_ref, sorted_ref):
    order = order_ref[...]
    many = positions // steps_before

    def one_position(spot, carry):
        pattern = pattern_ref[pl.program_id(0) * many + spot]
        for parity in range(2):
            rows = [ref[pattern, pl.ds(parity, half, stride=2), :] for ref in (near_ref, far_ref)]
            parts = split3(jnp.concatenate(rows, axis=1))
            sorted_ref[spot, parity * half : (parity + 1) * half, :] = sum(
                jnp.dot(part, order, preferred_element_type=f32) for part in parts
            )
        return carry

    lax.fori_loop(0, many, one_position, 0)


def sort_patterns(pattern, measured):
    return pl.pallas_call(
        sort_body,
        out_shape=jax.ShapeDtypeStruct((positions, win, win), f32),
        grid_spec=pltpu.PrefetchScalarGridSpec(
            num_scalar_prefetch=1,
            grid=(steps_before,),
            in_specs=[
                pl.BlockSpec((positions, win, half), lambda j, pattern: (0, 0, 0)),
                pl.BlockSpec((positions, win, half), lambda j, pattern: (0, 0, 1)),
                whole(win, win),
            ],
            out_specs=pl.BlockSpec((positions // steps_before, win, win), lambda j, pattern: (j, 0, 0)),
        ),
        cost_estimate=pl.CostEstimate(flops=2 * 3 * positions * win**3, bytes_accessed=4 << 20, transcendentals=0),
        name="sort_patterns",
    )(pattern, measured, measured, jnp.asarray(column_order()))


def prepare_body(starts_ref, probe_ref, parts_ref, rolled_ref, left_ref, right_ref):
    many = positions // steps_before

    def one_position(spot, carry):
        position = pl.program_id(0) * many + spot
        down = lax.rem(starts_ref[position, 0], 8)
        across = starts_ref[position, 1]
        kept = lax.broadcasted_iota(jnp.int32, (8, win), 0) >= down
        for plane in range(2):
            above = pltpu.roll(probe_ref[plane, win - 8 : win, :], down, axis=0)
            for row in range(0, win, 8):
                block = pltpu.roll(probe_ref[plane, row : row + 8, :], down, axis=0)
                rolled_ref[spot, plane, row : row + 8, :] = pltpu.roll(jnp.where(kept, block, above), across, axis=1)
                above = block
        for part, places in ((0, (0, 1)), (1, (2,))):
            table = parts_ref[spot, part]
            for place in places:
                left_ref[spot, :, place * win : (place + 1) * win] = table
                right_ref[spot, place * win : (place + 1) * win, :] = table
        return carry

    lax.fori_loop(0, many, one_position, 0)


def prepare(starts, probe):
    many = positions // steps_before
    return pl.pallas_call(
        prepare_body,
        out_shape=(
            jax.ShapeDtypeStruct((positions, 2, win, win), f32),
            jax.ShapeDtypeStruct((8, win, 3 * win), bf16),
            jax.ShapeDtypeStruct((8, 3 * win, win), bf16),
        ),
        grid_spec=pltpu.PrefetchScalarGridSpec(
            num_scalar_prefetch=1,
            grid=(steps_before,),
            in_specs=[
                whole(2, win, win),
                pl.BlockSpec((many, 2, win, win), lambda j, starts: (j, 0, 0, 0)),
            ],
            out_specs=[
                pl.BlockSpec((many, 2, win, win), lambda j, starts: (j, 0, 0, 0)),
                pl.BlockSpec((many, win, 3 * win), lambda j, starts: (j, 0, 0)),
                pl.BlockSpec((many, 3 * win, win), lambda j, starts: (j, 0, 0)),
            ],
        ),
        compiler_params=pltpu.CompilerParams(vmem_limit_bytes=44 << 20),
        cost_estimate=pl.CostEstimate(flops=positions * win**3, bytes_accessed=12 << 20, transcendentals=0),
        name="prepare",
    )(starts, probe, jnp.asarray(table_parts()))


def complex_mul(left_re, left_im, right_re, right_im):
    return (left_re * right_re - left_im * right_im, left_re * right_im + left_im * right_re)


def conj_mul(left_re, left_im, right_re, right_im):
    return (left_re * right_re + left_im * right_im, left_re * right_im - left_im * right_re)


def put_left(ref, side, row, value):
    high = value.astype(bf16)
    low = (value - high.astype(f32)).astype(bf16)
    size = value.shape[0]
    ref[side, row : row + size, :] = high
    ref[side, win + row : win + row + size, :] = low
    ref[side, 2 * win + row : 2 * win + row + size, :] = high


def put_right(ref, side, row, lane, value):
    high = value.astype(bf16)
    low = (value - high.astype(f32)).astype(bf16)
    size = value.shape[0]
    ref[side, row : row + size, lane : lane + half] = high
    ref[side, row : row + size, win + lane : win + lane + half] = low
    ref[side, row : row + size, 2 * win + lane : 2 * win + lane + half] = high


class Work:
    def __init__(self, starts_ref, position, wide, total, xa, xb, res):
        self.wide, self.total, self.xa, self.xb, self.res = wide, total, xa, xb, res
        a = starts_ref[position, 0]
        self.b = starts_ref[position, 1]
        self.offset = lax.rem(a, 8)
        self.base = pl.multiple_of(a - self.offset, 8)
        self.near = lax.broadcasted_iota(jnp.int32, (R, win), 1) >= self.b
        self.below = lax.broadcasted_iota(jnp.int32, (R, win), 0) >= self.offset

    def row_sets(self, row):
        first = (pl.ds(self.base + row, R), None)
        return (first,) if row else (first, (pl.ds(self.base + win, R), self.below))

    def window(self, plane, row):
        value = None
        for rows, mask in self.row_sets(row):
            block = jnp.where(self.near, self.wide[plane, rows, 0:win], self.wide[plane, rows, win : 2 * win])
            value = block if mask is None else jnp.where(mask, value, block)
        return value

    def add_window(self, plane, row, value):
        zero = jnp.zeros_like(value)
        for rows, mask in self.row_sets(row):
            part = value
            if row == 0:
                part = jnp.where(self.below, value, zero) if mask is None else jnp.where(self.below, zero, value)
            self.total[plane, rows, 0:win] += jnp.where(self.near, part, zero)
            self.total[plane, rows, win : 2 * win] += jnp.where(self.near, zero, part)

    def left_stage(self, table):
        for side in range(2):
            self.res[side] = jnp.dot(table[side], self.xa[side], preferred_element_type=f32)

    def right_stage(self, table):
        for side in range(2):
            self.res[side] = jnp.dot(self.xb[side], table[side], preferred_element_type=f32)

    def row_butterfly(self, row, upper, lower):
        for part in range(2):
            put_left(self.xa, 0, part * half + row, upper[part] + lower[part])
            put_left(self.xa, 1, part * half + row, upper[part] - lower[part])

    def lane_butterfly(self, row, field):
        for part in range(2):
            near_half, far_half = field[part][:, :half], field[part][:, half:]
            put_right(self.xb, 0, row, part * half, near_half + far_half)
            put_right(self.xb, 1, row, part * half, near_half - far_half)

    def lane_join(self, row):
        out = []
        for part in range(2):
            plus = self.res[0, row : row + R, part * half : (part + 1) * half]
            minus = self.res[1, row : row + R, part * half : (part + 1) * half]
            out.append(jnp.concatenate([plus + minus, plus - minus], axis=1))
        return out

    def row_join(self, row):
        plus = [self.res[0, part * half + row : part * half + row + R, :] for part in range(2)]
        minus = [self.res[1, part * half + row : part * half + row + R, :] for part in range(2)]
        return [p + m for p, m in zip(plus, minus)], [p - m for p, m in zip(plus, minus)]

    def rows_to_lanes(self):
        for row in range(0, half, R):
            upper, lower = self.row_join(row)
            self.lane_butterfly(row, upper)
            self.lane_butterfly(half + row, lower)

    def add_unrolled(self, target, source):
        up = jnp.where(self.offset == 0, 0, 8 - self.offset)
        across = jnp.where(self.b == 0, 0, win - self.b)
        kept = lax.broadcasted_iota(jnp.int32, (8, win), 0) < 8 - self.offset
        first = block = pltpu.roll(source[0:8, :], up, axis=0)
        for row in range(0, win, 8):
            below = pltpu.roll(source[row + 8 : row + 16, :], up, axis=0) if row + 8 < win else first
            target[row : row + 8, :] += pltpu.roll(jnp.where(kept, block, below), across, axis=1)
            block = below


def run_together(works):
    running, live = list(works), []
    while running or live:
        if running:
            live.append(running.pop(0))
        live = [w for w in live if next(w, "end") is None]


def assemble(flags_ref, wide, own_ref, ra_ref, rb_ref, ca_ref, cb_ref):
    row_odd, col_odd = flags_ref[0], flags_ref[1]
    wide[:, half_at(3 * (1 - row_odd)), half : half + win] = ra_ref[...]
    wide[:, half_at(3 * row_odd), half : half + win] = rb_ref[...]
    wide[:, 0 : 2 * win, half_at(3 * (1 - col_odd))] = ca_ref[...]
    wide[:, 0 : 2 * win, half_at(3 * col_odd)] = cb_ref[...]
    wide[:, half : half + win, half : half + win] = own_ref[...]


def give_out(flags_ref, total, wall_a, wall_b, mid):
    col_odd = flags_ref[1]
    wall_a[...] = total[:, 0 : 2 * win, half_at(3 * (1 - col_odd))]
    wall_b[...] = total[:, 0 : 2 * win, half_at(3 * col_odd)]
    mid[...] = total[:, 0 : 2 * win, half : half + win]


def propagate_body(
    starts_ref, flags_ref, own_ref, ra_ref, rb_ref, ca_ref, cb_ref, rolled_ref, left_ref, right_ref,
    phi_ref, wide, light, *slots,
):
    step = pl.program_id(0)

    @pl.when(step == 0)
    def _():
        assemble(flags_ref, wide, own_ref, ra_ref, rb_ref, ca_ref, cb_ref)
        light[...] = jnp.zeros_like(light)

    def work(slot):
        xa, xb, res, shares = slots[4 * slot : 4 * slot + 4]
        w = Work(starts_ref, at_once * step + slot, wide, None, xa, xb, res)
        for row in range(0, half, R):
            pair = []
            for at in (row, half + row):
                o_re, o_im = w.window(0, at), w.window(1, at)
                shares[0, at : at + R, :] = o_re * o_re + o_im * o_im
                probe = [rolled_ref[slot, part, at : at + R, :] for part in range(2)]
                pair.append(complex_mul(*probe, o_re, o_im))
            w.row_butterfly(row, *pair)
        yield
        w.left_stage(left_ref)
        w.add_unrolled(light, shares.at[0])
        yield
        w.rows_to_lanes()
        yield
        w.right_stage(right_ref)
        yield
        for row in range(0, win, R):
            phi_ref[slot, 0, row : row + R, :], phi_ref[slot, 1, row : row + R, :] = w.lane_join(row)
        yield

    run_together(work(slot) for slot in range(at_once))


def detect_body(
    starts_ref, flags_ref, own_ref, ra_ref, rb_ref, ca_ref, cb_ref, phi_ref, sorted_ref,
    left_ref, right_ref, left_back, right_back,
    inner_ref, wall_a, wall_b, mid, wide, total, *slots,
):
    step = pl.program_id(0)

    @pl.when(step == 0)
    def _():
        assemble(flags_ref, wide, own_ref, ra_ref, rb_ref, ca_ref, cb_ref)
        total[...] = jnp.zeros_like(total)

    def work(slot):
        xa, xb, res = slots[4 * slot : 4 * slot + 3]
        w = Work(starts_ref, at_once * step + slot, wide, total, xa, xb, res)

        def phi(row):
            return [phi_ref[slot, part, row : row + R, :] for part in range(2)]

        for row in range(0, half, R):
            pair = [complex_mul(*phi(at), w.window(0, at), w.window(1, at)) for at in (row, half + row)]
            w.row_butterfly(row, *pair)
        yield
        w.left_stage(left_ref)
        yield
        for side in range(2):
            for row in range(0, half, R):
                w.lane_butterfly(
                    side * half + row, [res[side, part * half + row : part * half + row + R, :] for part in range(2)]
                )
        yield
        w.right_stage(right_ref)
        yield
        for side in range(2):
            for row in range(0, win, R):
                far_re = res[side, row : row + R, 0:half]
                far_im = res[side, row : row + R, half:win]
                amplitude = sorted_ref[slot, row : row + R, side * half : (side + 1) * half]
                factor = 1.0 - amplitude * lax.rsqrt(far_re * far_re + far_im * far_im + 1.0)
                put_right(xb, side, row, 0, factor * far_re)
                put_right(xb, side, row, half, factor * far_im)
        yield
        w.right_stage(right_back)
        yield
        for side in range(2):
            for row in range(0, half, R):
                field = w.lane_join(side * half + row)
                for part in range(2):
                    put_left(xa, side, part * half + row, field[part])
        yield
        w.left_stage(left_back)
        yield
        for row in range(0, half, R):
            for at, back in zip((row, half + row), w.row_join(row)):
                for part, term in enumerate(conj_mul(*phi(at), *back)):
                    w.add_window(part, at, term)
                inner = conj_mul(w.window(0, at), w.window(1, at), *back)
                inner_ref[slot, 0, at : at + R, :], inner_ref[slot, 1, at : at + R, :] = inner
        yield

    run_together(work(slot) for slot in range(at_once))

    @pl.when(step == positions // at_once - 1)
    def _():
        give_out(flags_ref, total, wall_a, wall_b, mid)


def return_body(
    starts_ref, flags_ref, wide, inner_ref, rolled_ref, light, left_ref, right_ref,
    wall_a, wall_b, mid, keep, send, total, share, *slots,
):
    step = pl.program_id(0)

    @pl.when(step == 0)
    def _():
        total[...] = jnp.zeros_like(total)
        share[0:2] = jnp.zeros((2, win, win), f32)
        share[2] = light[...]

    def work(slot):
        xa, xb, res, shares = slots[4 * slot : 4 * slot + 4]
        w = Work(starts_ref, at_once * step + slot, wide, total, xa, xb, res)
        for row in range(0, half, R):
            pair = [[inner_ref[slot, part, at : at + R, :] for part in range(2)] for at in (row, half + row)]
            w.row_butterfly(row, *pair)
        yield
        w.left_stage(left_ref)
        yield
        w.rows_to_lanes()
        yield
        w.right_stage(right_ref)
        yield
        for at in range(0, win, R):
            entry = w.lane_join(at)
            probe = [rolled_ref[slot, part, at : at + R, :] for part in range(2)]
            for part, term in enumerate(conj_mul(*probe, *entry)):
                w.add_window(part, at, term)
            terms = conj_mul(w.window(0, at), w.window(1, at), *entry)
            shares[0, at : at + R, :], shares[1, at : at + R, :] = terms
        for part in range(2):
            w.add_unrolled(share.at[part], shares.at[part])
        yield

    run_together(work(slot) for slot in range(at_once))

    @pl.when(step == positions // at_once - 1)
    def _():
        give_out(flags_ref, total, wall_a, wall_b, mid)
        keep[...] = share[:, half_at(flags_ref[1]), :]
        send[...] = share[:, half_at(1 - flags_ref[1]), :]


def position_kernel(body, products, starts, flags, inputs, outputs, scratch):
    def spec(shape, kind):
        if kind == "each":
            return pl.BlockSpec((at_once,) + shape[1:], lambda j, *_: (j,) + (0,) * (len(shape) - 1))
        if kind == "whole":
            return whole(*shape)
        return pl.BlockSpec((2,) + shape[1:], lambda j, *_: (kind,) + (0,) * (len(shape) - 1))

    slot = [
        pltpu.VMEM((2, 3 * win, win), bf16),
        pltpu.VMEM((2, win, 3 * win), bf16),
        pltpu.VMEM((2, win, win), f32),
        pltpu.VMEM((2, win, win), f32),
    ]
    return pl.pallas_call(
        body,
        out_shape=[jax.ShapeDtypeStruct(shape, f32) for shape, _ in outputs],
        grid_spec=pltpu.PrefetchScalarGridSpec(
            num_scalar_prefetch=2,
            grid=(positions // at_once,),
            in_specs=[spec(x.shape, kind) for x, kind in inputs],
            out_specs=[spec(shape, kind) for shape, kind in outputs],
            scratch_shapes=scratch + slot * at_once,
        ),
        compiler_params=pltpu.CompilerParams(vmem_limit_bytes=44 << 20),
        cost_estimate=pl.CostEstimate(
            flops=products * 24 * positions * win**3, bytes_accessed=products * (8 << 20), transcendentals=0
        ),
    )(starts, flags, *(x for x, _ in inputs))


def whole(*shape):
    return pl.BlockSpec(shape, lambda *ids: (0,) * len(shape))


def small_kernel(kernel, flags, inputs, shapes):
    size = sum(x.size for x in inputs) + sum(math.prod(shape) for shape in shapes)
    return pl.pallas_call(
        kernel,
        out_shape=[jax.ShapeDtypeStruct(shape, f32) for shape in shapes],
        grid_spec=pltpu.PrefetchScalarGridSpec(
            num_scalar_prefetch=1,
            grid=(1,),
            in_specs=[whole(*x.shape) for x in inputs],
            out_specs=[whole(*shape) for shape in shapes],
        ),
        compiler_params=pltpu.CompilerParams(vmem_limit_bytes=48 << 20),
        cost_estimate=pl.CostEstimate(flops=size, bytes_accessed=4 * size, transcendentals=0),
    )(flags, *inputs)


def half_at(choice):
    return pl.ds(pl.multiple_of(choice * half, half), half)


def pack_walls(flags_ref, two_ref, ra_ref, rb_ref, a_ref, b_ref):
    row_odd, col_odd = flags_ref[0], flags_ref[1]
    for out, lanes in ((a_ref, half_at(1 - col_odd)), (b_ref, half_at(col_odd))):
        out[:, half : half + win, :] = two_ref[:, :, lanes]
        out[:, half_at(3 * (1 - row_odd)), :] = ra_ref[:, :, lanes]
        out[:, half_at(3 * row_odd), :] = rb_ref[:, :, lanes]


def fold_walls(flags_ref, mid_ref, qa_ref, qb_ref, a_ref, b_ref, center_ref):
    row_odd, col_odd = flags_ref[0], flags_ref[1]
    for got, lanes in ((qa_ref, half_at(1 - col_odd)), (qb_ref, half_at(col_odd))):
        center_ref[:, :, lanes] = mid_ref[:, half : half + win, lanes] + got[:, half : half + win, :]
        for out, rows in ((a_ref, half_at(3 * (1 - row_odd))), (b_ref, half_at(3 * row_odd))):
            out[:, :, lanes] = mid_ref[:, rows, lanes] + got[:, rows, :]


def fold_rows(flags_ref, center_ref, a_ref, b_ref, out_ref):
    odd = flags_ref[0]
    for got, rows in ((a_ref, half_at(1 - odd)), (b_ref, half_at(odd))):
        out_ref[:, rows, :] = center_ref[:, rows, :] + got[...]


def pack_share(flags_ref, keep_ref, got_ref, out_ref):
    for tile in range(64):
        for plane, spot in ((tile // 32, 0), (2, 8)):
            rows = slice(tile % 32 // 2 * 8, tile % 32 // 2 * 8 + 8)
            lanes = slice(tile % 2 * half, tile % 2 * half + half)
            out_ref[tile, spot : spot + 8, :] = keep_ref[plane, rows, lanes] + got_ref[plane, rows, lanes]


def take_step(flags_ref, parts_ref, out_ref):
    total = parts_ref[0]
    for tile in range(1, 64):
        total = total + parts_ref[tile]
    step = total[0:8] * lax.rsqrt(total[8:16] + 1.0)
    for tile in range(64):
        out_ref[tile] = step


def join_step(flags_ref, own_ref, other_ref, out_ref):
    odd = flags_ref[1]
    for tile in range(64):
        row = tile % 32 // 2 * 8
        lanes = slice(tile % 2 * half, tile % 2 * half + half)
        out_ref[tile // 32, pl.ds(pl.multiple_of(odd * half + row, 8), 8), lanes] = own_ref[tile]
        out_ref[tile // 32, pl.ds(pl.multiple_of((1 - odd) * half + row, 8), 8), lanes] = other_ref[tile]


def swapped(block, axis, first):
    pairs = [(i, i + 1) for i in range(first, lax.axis_size(axis) - 1, 2)]
    return lax.ppermute(block, axis, pairs + [(j, i) for i, j in pairs])


def exchanged(parts):
    rows, cols = lax.axis_size("row"), lax.axis_size("col")
    groups = [[r * cols + c for r in range(rows) for c in range(odd, cols, 2)] for odd in range(2)]
    return lax.all_to_all(parts, ("row", "col"), 0, 0, axis_index_groups=groups, tiled=True)


def gradients(object_one, object_two, probe, scan_pos, pattern_index, measured):
    starts = scan_pos[0, 0]
    flags = jnp.stack([lax.axis_index("row") % 2, lax.axis_index("col") % 2]).astype(jnp.int32)
    edge, wall, tile = (2, half, win), (2, 2 * win, half), (2, win, win)

    def edges_of(own):
        zero = jnp.zeros((), jnp.int32)
        ra, rb = (lax.dynamic_slice(own, (zero, half * at, zero), edge) for at in (1 - flags[0], flags[0]))
        return swapped(ra, "row", 0), swapped(rb, "row", 1)

    def walls_of(own, edges):
        ca, cb = small_kernel(pack_walls, flags, (own,) + edges, (wall, wall))
        return swapped(ca, "col", 0), swapped(cb, "col", 1)

    def folded(wa, wb, mid):
        wa = swapped(wa, "col", 0)
        wb = swapped(wb, "col", 1)
        ga, gb, center = small_kernel(fold_walls, flags, (mid, wa, wb), (edge, edge, tile))
        ga = swapped(ga, "row", 0)
        gb = swapped(gb, "row", 1)
        return small_kernel(fold_rows, flags, (center, ga, gb), (tile,))[0]

    edges_one, edges_two = edges_of(object_one), edges_of(object_two)
    walls_one = walls_of(object_one, edges_one)
    walls_two = walls_of(object_two, edges_two)
    ordered = sort_patterns(pattern_index[0, 0], measured[0, 0])
    rolled, ltab, rtab = prepare(starts, probe)
    stack, wide_shape = (positions, 2, win, win), (2, 2 * win + 8, 2 * win)
    parts = (wall, "whole"), (wall, "whole"), ((2, 2 * win, win), "whole")
    pieces = [(x, "whole") for x in (object_one,) + edges_one + walls_one]
    phi, wide, light = position_kernel(
        propagate_body, 1, starts, flags,
        pieces + [(rolled, "each"), (ltab, 2), (rtab, 0)],
        [(stack, "each"), (wide_shape, "whole"), ((win, win), "whole")], [],
    )
    pieces = [(x, "whole") for x in (object_two,) + edges_two + walls_two]
    inner, *two = position_kernel(
        detect_body, 2, starts, flags,
        pieces + [(phi, "each"), (ordered, "each"), (ltab, 3), (rtab, 1), (ltab, 1), (rtab, 3)],
        [(stack, "each"), *parts], [pltpu.VMEM(wide_shape, f32), pltpu.VMEM(wide_shape, f32)],
    )
    *one, keep, send = position_kernel(
        return_body, 1, starts, flags,
        [(wide, "whole"), (inner, "each"), (rolled, "each"), (light, "whole"), (ltab, 0), (rtab, 2)],
        [*parts, ((3, half, win), "whole"), ((3, half, win), "whole")],
        [pltpu.VMEM(wide_shape, f32), pltpu.VMEM((3, win, win), f32)],
    )
    share = small_kernel(pack_share, flags, (keep, swapped(send, "col", 0)), ((64, 16, half),))[0]
    grad_two = folded(*two)
    grad_one = folded(*one)
    step = small_kernel(take_step, flags, (exchanged(share),), ((64, 8, half),))[0]
    step = exchanged(step)
    probe_step = small_kernel(join_step, flags, (step, swapped(step, "col", 0)), (tile,))[0]
    return (grad_one, grad_two, probe_step)


def solution(mesh):
    placed = (
        P(None, "row", "col"),
        P(None, "row", "col"),
        P(),
        P("row", "col", None, None),
        P("row", "col", None),
        P("row", "col", None, None, None),
    )
    return jax.shard_map(
        gradients,
        mesh=mesh,
        in_specs=placed,
        out_specs=(P(None, "row", "col"), P(None, "row", "col"), P()),
        check_vma=False,
    )
```
